512 devices in a mesh: dp: 16 (over z), expert: 32 (over y, x, core).
Axes of the slice: x: 4, y: 4, z: 16, core: 2. Of those that a mesh axis runs over, the one named last changes fastest.
Arguments:
- tokens: bfloat16 [2048, 4096], P('dp', 'expert'), may hold values from -6 to 6
- norm_gain: float32 [4096], replicated, may hold values from 0.1 to 1.9
- routes: int32 [2048, 2], P('dp'), may hold values from 0 to 31, all different within a row; in each aligned block of 128 rows (0 to 127, 128 to 255, ...) at most 10 rows name the same one
- route_prob: float32 [2048, 2], P('dp'), may hold values from 0.2 to 1
- gate_weight: bfloat16 [32, 4096, 2048], P('expert', None, 'dp'), may hold values from -0.09375 to 0.09375
- up_weight: bfloat16 [32, 4096, 2048], P('expert', None, 'dp'), may hold values from -0.09375 to 0.09375
- down_weight: bfloat16 [32, 2048, 4096], P('expert', 'dp'), may hold values from -0.125 to 0.125
- key_value_weight: bfloat16 [4096, 2048], P('expert'), may hold values from -0.09375 to 0.09375
- key_value_target: bfloat16 [2048, 2048], P('dp', 'expert'), may hold values from -6 to 6
- concept_mask: int32 [2048], P('dp'), may hold values 0 or 1
Outputs:
- down_grad: bfloat16 [32, 2048, 4096], P('expert', 'dp')
- key_value_grad: float32 [4096, 2048], P('expert', 'dp')
The draws below stay inside these ranges and needn't reach their ends.
Inputs may be any that keep to these rules, and one draw needn't show every extreme that they name: `routes`: in each aligned block of 128 rows no expert is named by more than 10 rows; the two choices of a token differ.
All inputs are finite; a program needn't handle non-finite values. No bound on the sum of `concept_mask` on one device may be relied on, other than what follows from the above.
Results may differ from the reference program's by a relative error of at most 0.033.
Values may be sent and summed in bfloat16 or wider, within the bound.
No kernel may reach another device: no remote copies, remote signals or barrier semaphores. Data moves between devices by JAX's collectives and lax.ppermute only.
A program may use at most 64 MiB of HBM per device.

```python
import math
import jax
import jax.numpy as jnp
import numpy as np
from jax import lax

D = 4096
KV = 1024
FF_DEV = 128
TOP = 2
TOK = 128
FF = 2048
EXPERTS = 32
CAP = 10
TOKENS = 2048
N_DP = 16
N_EXPERT = 32


def place_ends(entries, own_key, smallest, high):
    longest = entries.shape.index(max(entries.shape))
    spots = []
    for shift in (0, 1):
        where = [jax.random.randint(jax.random.fold_in(own_key, axis), (), 0, length) for axis, length in enumerate(entries.shape)]
        where[longest] = (where[longest] + shift) % entries.shape[longest]
        spots.append(tuple(where))
    return entries.at[spots[0]].set(smallest).at[spots[1]].set(high)


def block_levels(own_key, dims, cuts, smallest, top_value):
    loudness = 1.0
    for dim, shards_of in cuts:
        steps = jax.random.uniform(jax.random.fold_in(jax.random.fold_in(own_key, 6), dim), (shards_of,), jnp.float32, smallest / len(cuts), top_value / len(cuts))
        loudness = loudness * jnp.repeat(jnp.exp(steps), dims[dim] // shards_of).reshape((-1,) + (1,) * (len(dims) - 1 - dim))
    return loudness


def assign_block(rng, own, number, rows, number_of, top, limit, slope):
    ranking = jax.random.permutation(rng, number_of)
    heavy_load, usual = shares(number_of, rows * top, limit, slope, True), shares(number_of, rows * top, limit, slope, False)
    places = jnp.arange(number_of)

    def named(lengths, turn):
        used = int((lengths > 0).sum())
        fixed = max(1, used // 4)
        moved = fixed + (places - fixed + turn * (used - fixed)) % max(1, number_of - fixed)
        return jnp.zeros((number_of,), jnp.int32).at[ranking[jnp.where(places < fixed, places, moved)]].set(jnp.asarray(lengths, jnp.int32))

    lengths = jnp.where(number % 4 == 0, named(heavy_load, number // 4), named(usual, number - number // 4 - 1))
    mixed = jax.random.permutation(jax.random.fold_in(own, 3), number_of)
    giver, receiver = mixed[0:number_of // 2 * 2:2], mixed[1:number_of // 2 * 2:2]
    room = jnp.minimum(lengths[giver] - 1, limit - lengths[receiver]) // 2
    room = jnp.where((giver == ranking[0]) | (receiver == ranking[0]) | (lengths[receiver] == 0), 0, jnp.maximum(room, 0))
    moved = jax.random.randint(jax.random.fold_in(own, 4), (number_of // 2,), 0, 1 << 20) % (room + 1)
    lengths = lengths.at[giver].add(-moved).at[receiver].add(moved)
    members = jnp.searchsorted(jnp.cumsum(lengths), jnp.arange(rows * top), side="right").astype(jnp.int32)
    table = members.reshape(top, rows).T
    table = table[jax.random.permutation(jax.random.fold_in(own, 1), rows)]
    turn = jax.random.randint(jax.random.fold_in(own, 2), (rows, 1), 0, top)
    return jnp.take_along_axis(table, (jnp.arange(top)[None, :] + turn) % top, axis=1)


def shares(number_of, total, most, lean, full):
    portions = [(1 << 20) // math.isqrt(grade ** lean) + 1 for grade in range(1, number_of + 1)]
    largest = most if full else min(most, max(-(-total // number_of), total * portions[0] // sum(portions)))
    least = 1 if total - largest >= number_of - 1 else 0
    given, surplus = [largest] + [least] * (number_of - 1), total - largest - least * (number_of - 1)
    while surplus > 0:
        candidates = [i for i in range(1, number_of) if given[i] < largest] or [i for i in range(1, number_of) if given[i] < most]
        pool, left = sum([portions[i] for i in candidates]), surplus
        for i in candidates:
            more = min(most - given[i], max(1, left * portions[i] // pool), surplus)
            given[i] = given[i] + more
            surplus = surplus - more
    return np.array(given)


def centred(key, dims, deviation, bound, cuts=(), held_as=jnp.bfloat16):
    entries = deviation * jax.random.normal(key, dims, jnp.float32)
    if cuts:
        entries = entries * block_levels(key, dims, cuts, -0.22, 0.18)
    return jnp.clip(entries, -bound, bound).astype(held_as)


def setup_inputs(seed: int = 0) -> dict:
    streams_of = jax.random.split(jax.random.key(seed), 11)
    tokens = centred(streams_of[0], (TOKENS, D), 1.0, 6.0, ((0, 16), (1, 32)))
    norm_gain = jnp.clip(1.0 + 0.18 * jax.random.normal(streams_of[1], (D,), jnp.float32), 0.1, 1.9)
    routes_keys = jax.random.split(jax.random.fold_in(streams_of[2], 1), TOKENS // TOK)
    routes_turns = jax.random.permutation(jax.random.fold_in(streams_of[2], 3), TOKENS // TOK)
    routes = jax.vmap(lambda own, number: assign_block(jax.random.fold_in(streams_of[2], 2), own, number, TOK, EXPERTS, TOP, CAP, 2))(routes_keys, routes_turns).reshape((TOKENS, TOP))
    route_prob = jnp.clip(0.2 + 0.8 * jax.random.uniform(streams_of[3], (TOKENS, TOP), jnp.float32) ** block_levels(streams_of[3], (TOKENS, TOP), ((0, 16),), -0.2, 0.2), 0.2, 1.0)
    gate_weight = centred(streams_of[4], (EXPERTS, D, FF), D ** -0.5, 0.09375, ((0, 32), (2, 16)))
    up_weight = centred(streams_of[5], (EXPERTS, D, FF), D ** -0.5, 0.09375, ((0, 32), (2, 16)))
    down_weight = centred(streams_of[6], (EXPERTS, FF, D), FF ** -0.5, 0.125, ((0, 32), (1, 16)))
    key_value_weight = centred(streams_of[7], (D, 2 * KV), D ** -0.5, 0.09375, ((0, 32),))
    key_value_target = centred(streams_of[8], (TOKENS, 2 * KV), 1.0, 6.0, ((0, 16), (1, 32)))
    concept_mask = place_ends((jax.random.randint(streams_of[9], (TOKENS,), 0, 2) < 1).astype(jnp.int32), jax.random.fold_in(streams_of[9], 1), 0, 1)
    return dict(tokens=tokens, norm_gain=norm_gain, routes=routes, route_prob=route_prob, gate_weight=gate_weight, up_weight=up_weight, down_weight=down_weight, key_value_weight=key_value_weight, key_value_target=key_value_target, concept_mask=concept_mask)


def slot_numbers(block_routes):
    flat = block_routes.reshape(-1)
    onehot = (flat[:, None] == jnp.arange(EXPERTS, dtype=jnp.int32)[None, :]).astype(jnp.int32)
    before = jnp.cumsum(onehot, axis=0) - onehot
    return (flat, lax.optimization_barrier(jnp.sum(before * onehot, axis=1)).astype(jnp.int32))

def reference(tokens, norm_gain, routes, route_prob, gate_weight, up_weight, down_weight, key_value_weight, key_value_target, concept_mask):
    slot_total = N_DP * CAP
    values = tokens.astype(jnp.float32)
    mean_sq = lax.optimization_barrier(jnp.mean(values * values, axis=1, keepdims=True))
    normed = (values * lax.rsqrt(mean_sq + 1e-06) * norm_gain[None, :]).astype(jnp.bfloat16)
    chosen, slot = jax.vmap(slot_numbers)(routes.reshape(N_DP, TOK, TOP))
    block_id = jnp.arange(N_DP, dtype=jnp.int32)[:, None]
    position = (chosen * slot_total + block_id * CAP + slot).reshape(-1).astype(jnp.int32)
    token_of = (jnp.arange(TOKENS * TOP, dtype=jnp.int32) // TOP).astype(jnp.int32)
    slot_rows = jnp.zeros((EXPERTS * slot_total, D), jnp.bfloat16).at[position].set(normed[token_of])
    slot_rows = slot_rows.reshape(EXPERTS, slot_total, D)

    def expert_forward(group):
        rows_in, gate_mat, up_mat, down_mat = group
        gate_val = jnp.dot(rows_in, gate_mat, preferred_element_type=jnp.float32)
        up_val = jnp.dot(rows_in, up_mat, preferred_element_type=jnp.float32)
        hidden = (jax.nn.silu(gate_val) * up_val).astype(jnp.bfloat16)
        pieces = jnp.einsum('rjf,jfd->jrd', hidden.reshape(slot_total, N_DP, FF_DEV).astype(jnp.float32), down_mat.reshape(N_DP, FF_DEV, D).astype(jnp.float32))
        rounded = lax.optimization_barrier(pieces.astype(jnp.bfloat16))
        return (hidden, lax.optimization_barrier(jnp.sum(rounded.astype(jnp.float32), axis=0)).astype(jnp.bfloat16))
    hidden_all, expert_out = lax.map(expert_forward, (slot_rows, gate_weight, up_weight, down_weight))
    prob_flat = route_prob.reshape(-1)
    picked = expert_out.reshape(EXPERTS * slot_total, D)[position].astype(jnp.float32) * prob_flat[:, None]
    expert_mix = picked.reshape(TOKENS, TOP, D).sum(axis=1)
    state = (values + expert_mix).astype(jnp.bfloat16)
    width = D // N_EXPERT
    state_blocks = state.reshape(TOKENS, N_EXPERT, width).transpose(1, 0, 2)
    weight_blocks = key_value_weight.reshape(N_EXPERT, width, 2 * KV)

    def add_block(total, group):
        piece = jnp.dot(group[0], group[1], preferred_element_type=jnp.float32).astype(jnp.bfloat16)
        piece = lax.optimization_barrier(piece)
        return (total + piece.astype(jnp.float32), None)
    key_value, unused = lax.scan(add_block, jnp.zeros((TOKENS, 2 * KV), jnp.float32), (state_blocks, weight_blocks))
    mask_col = concept_mask.astype(jnp.float32)[:, None]
    cotangent = (mask_col * (key_value - key_value_target.astype(jnp.float32)) * TOK ** (-0.5)).astype(jnp.bfloat16)

    def add_grad(total, group):
        piece = jnp.dot(group[0].T, group[1], preferred_element_type=jnp.float32).astype(jnp.bfloat16)
        piece = lax.optimization_barrier(piece)
        return (total + piece.astype(jnp.float32), None)
    key_value_grad, unused2 = lax.scan(add_grad, jnp.zeros((D, 2 * KV), jnp.float32), (state.reshape(N_DP, TOK, D), cotangent.reshape(N_DP, TOK, 2 * KV)))
    state_grad = jnp.dot(cotangent, key_value_weight.T, preferred_element_type=jnp.float32)
    row_grad = (state_grad[token_of] * prob_flat[:, None]).astype(jnp.bfloat16)
    slot_grad = jnp.zeros((EXPERTS * slot_total, D), jnp.bfloat16).at[position].set(row_grad)
    slot_grad = slot_grad.reshape(EXPERTS, slot_total, D)

    def expert_grad(group):
        return jnp.dot(group[0].T, group[1], preferred_element_type=jnp.float32).astype(jnp.bfloat16)
    down_grad = lax.map(expert_grad, (hidden_all, slot_grad))
    return (down_grad, key_value_grad)
```

```python
import jax
import jax.numpy as jnp
from jax import lax
from jax.experimental import pallas as pl
from jax.experimental.pallas import tpu as pltpu
from jax.sharding import PartitionSpec as P

f32 = jnp.float32
bf16 = jnp.bfloat16
eps_norm = 1e-06
meta_rows = 16
group = 4


def call(body, outs, *operands):
    vmem = pl.BlockSpec(memory_space=pltpu.VMEM)
    single = not isinstance(outs, (list, tuple))
    return pl.pallas_call(
        body,
        out_shape=outs,
        in_specs=[vmem] * len(operands),
        out_specs=vmem if single else [vmem] * len(outs),
        compiler_params=pltpu.CompilerParams(vmem_limit_bytes=56 * 1024 * 1024),
    )(*operands)


def iota(shape, axis):
    return lax.broadcasted_iota(jnp.int32, shape, axis)


def contract(a, b, da, db):
    return lax.dot_general(a, b, (((da,), (db,)), ((), ())), preferred_element_type=f32)


def prepare(tok_ref, routes_ref, prob_ref, out_ref):
    rows, experts = tok_ref.shape[0], 32
    out_ref[0:rows, :] = tok_ref[...]
    lane = iota((rows, rows), 1)
    routes = routes_ref[...].astype(f32)
    prob = prob_ref[...]
    table = jnp.where(
        lane == 0,
        routes[:, 0:1],
        jnp.where(
            lane == 1,
            routes[:, 1:2],
            jnp.where(lane == 2, prob[:, 0:1], jnp.where(lane == 3, prob[:, 1:2], 0.0)),
        ),
    )
    table = table.T
    first, second = table[0:1, :], table[1:2, :]
    names = iota((experts, rows), 0).astype(f32)
    is_first, is_second = names == first, names == second
    named = jnp.where(is_first | is_second, 1.0, 0.0).astype(bf16)
    earlier = jnp.where(iota((rows, rows), 0) < lane, 1.0, 0.0).astype(bf16)
    before = jnp.dot(named, earlier, preferred_element_type=f32)
    slot_first = jnp.sum(jnp.where(is_first, before, 0.0), axis=0, keepdims=True)
    slot_second = jnp.sum(jnp.where(is_second, before, 0.0), axis=0, keepdims=True)
    row = iota((meta_rows, rows), 0)
    meta = jnp.where(
        row == 0,
        first,
        jnp.where(
            row == 1,
            second,
            jnp.where(
                row == 2,
                slot_first,
                jnp.where(
                    row == 3,
                    slot_second,
                    jnp.where(row == 4, table[2:3, :], jnp.where(row == 5, table[3:4, :], 0.0)),
                ),
            ),
        ),
    )
    out_ref[rows : rows + meta_rows, :] = meta.astype(bf16)


def selection(meta, inner, capacity, weighted):
    tall = group * capacity
    at = [
        (meta[k : k + 1] * tall + inner * capacity + meta[2 + k : 3 + k]).astype(jnp.int32)
        for k in (0, 1)
    ]
    slots = iota((32 * tall, meta.shape[1]), 0)
    if weighted:
        picked = jnp.where(slots == at[0], meta[4:5], jnp.where(slots == at[1], meta[5:6], 0.0))
    else:
        picked = jnp.where((slots == at[0]) | (slots == at[1]), 1.0, 0.0)
    return picked.astype(bf16)


def block_meta(gathered_ref, block, rows):
    return gathered_ref[block, rows : rows + meta_rows, :].astype(f32)


def dispatch(gathered_ref, out_ref):
    blocks, rows = gathered_ref.shape[0], gathered_ref.shape[1] - meta_rows
    capacity = out_ref.shape[1] // blocks
    tall = group * capacity
    for g in range(blocks // group):
        total = 0.0
        for inner in range(group):
            block = g * group + inner
            chosen = selection(block_meta(gathered_ref, block, rows), inner, capacity, False)
            total = total + jnp.dot(
                chosen, gathered_ref[block, 0:rows, :], preferred_element_type=f32
            )
        for e in range(out_ref.shape[0]):
            out_ref[e, g * tall : (g + 1) * tall, :] = total[e * tall : (e + 1) * tall].astype(bf16)


def dispatch_grad(gathered_ref, grad_ref, out_ref):
    blocks, rows = gathered_ref.shape[0], gathered_ref.shape[1] - meta_rows
    capacity = out_ref.shape[1] // blocks
    tall = group * capacity
    for g in range(blocks // group):
        total = 0.0
        for inner in range(group):
            block = g * group + inner
            chosen = selection(block_meta(gathered_ref, block, rows), inner, capacity, True)
            total = total + contract(chosen, grad_ref[block], 1, 1)
        for e in range(out_ref.shape[0]):
            out_ref[e, g * tall : (g + 1) * tall, :] = total[e * tall : (e + 1) * tall].astype(bf16)


def expert(rows_ref, gain_ref, gate_ref, up_ref, down_ref, out_ref, hidden_ref):
    parts, width = rows_ref.shape[0], rows_ref.shape[2]
    values = jnp.concatenate([rows_ref[p] for p in range(parts)], axis=1).astype(f32)
    mean_sq = jnp.sum(values * values, axis=1, keepdims=True) / (parts * width)
    normed = (values * lax.rsqrt(mean_sq + eps_norm) * gain_ref[...]).astype(bf16)
    gate_val = jnp.dot(normed, gate_ref[...], preferred_element_type=f32)
    up_val = jnp.dot(normed, up_ref[...], preferred_element_type=f32)
    hidden = (gate_val / (1.0 + jnp.exp(-gate_val)) * up_val).astype(bf16)
    hidden_ref[...] = hidden
    product = jnp.dot(hidden, down_ref[...], preferred_element_type=f32)
    for p in range(parts):
        out_ref[p] = product[:, p * width : (p + 1) * width].astype(bf16)


def combine(gathered_ref, back_ref, out_ref):
    blocks, rows = gathered_ref.shape[0], gathered_ref.shape[1] - meta_rows
    capacity = back_ref.shape[1] // blocks
    tall = group * capacity
    for g in range(blocks // group):
        back = jnp.concatenate(
            [back_ref[e, g * tall : (g + 1) * tall, :].astype(f32) for e in range(back_ref.shape[0])],
            axis=0,
        )
        back = back.T.astype(bf16)
        for inner in range(group):
            block = g * group + inner
            chosen = selection(block_meta(gathered_ref, block, rows), inner, capacity, True)
            out_ref[block] = jnp.dot(back, chosen, preferred_element_type=f32).astype(bf16)


def project(pieces_ref, tok_ref, weight_ref, state_ref, out_ref):
    total = tok_ref[...].astype(f32).T
    for p in range(pieces_ref.shape[0]):
        total = total + pieces_ref[p].astype(f32)
    state = total.astype(bf16)
    state_ref[...] = state
    out_ref[...] = contract(weight_ref[...], state, 0, 0).astype(bf16)


def form_cotangent(pieces_ref, target_ref, mask_ref, out_ref):
    total = pieces_ref[0].astype(f32)
    for p in range(1, pieces_ref.shape[0]):
        total = total + pieces_ref[p].astype(f32)
    target = target_ref[...].astype(f32)
    rows = target.shape[0]
    target = jnp.concatenate([target, target], axis=1).T[0 : target.shape[1]]
    scaled = mask_ref[...].astype(f32) * (total - target) * rows ** (-0.5)
    scaled = scaled.astype(bf16)
    for p in range(out_ref.shape[0]):
        out_ref[p] = scaled


def gradients(cot_ref, state_ref, weight_ref, state_grad_ref, pieces_ref):
    state_grad_ref[...] = jnp.dot(
        weight_ref[...], cot_ref[...], preferred_element_type=f32
    ).astype(bf16)
    state = state_ref[...]
    width = cot_ref.shape[0] // pieces_ref.shape[0]
    for p in range(pieces_ref.shape[0]):
        pieces_ref[p] = contract(state, cot_ref[p * width : (p + 1) * width, :], 1, 1).astype(bf16)


def down_gradient(hidden_ref, rows_ref, out_ref):
    hidden = hidden_ref[...].astype(f32).T.astype(bf16)
    width = rows_ref.shape[2]
    for p in range(rows_ref.shape[0]):
        out_ref[:, p * width : (p + 1) * width] = jnp.dot(
            hidden, rows_ref[p], preferred_element_type=f32
        ).astype(bf16)


def per_device(
    tokens,
    norm_gain,
    routes,
    route_prob,
    gate_weight,
    up_weight,
    down_weight,
    key_value_weight,
    key_value_target,
    concept_mask,
):
    rows, width = tokens.shape
    experts = lax.axis_size("expert")
    blocks = lax.axis_size("dp")
    capacity = 5 * rows * routes.shape[1] // (4 * experts)
    keys = key_value_weight.shape[1]

    def shape(*dims, dtype=bf16):
        return jax.ShapeDtypeStruct(dims, dtype)

    def exchange(value, axis):
        return lax.all_to_all(value, axis, split_axis=0, concat_axis=0, tiled=True)

    packed = call(prepare, shape(rows + meta_rows, width), tokens, routes, route_prob)
    gathered = lax.all_gather(packed, "dp", axis=0)
    slots = shape(experts, blocks * capacity, width)
    arrived = exchange(call(dispatch, slots, gathered), "expert")
    out_rows, hidden = call(
        expert,
        [slots, shape(blocks * capacity, gate_weight.shape[2])],
        arrived,
        norm_gain[None, :],
        gate_weight[0],
        up_weight[0],
        down_weight[0],
    )
    returned = exchange(out_rows, "expert")
    mixed = exchange(call(combine, shape(blocks, width, rows), gathered, returned), "dp")
    state, proj = call(
        project, [shape(width, rows), shape(keys, rows)], mixed, tokens, key_value_weight
    )
    proj = exchange(proj.reshape(experts, keys // experts, rows), "expert")
    spread = call(form_cotangent, shape(*proj.shape), proj, key_value_target, concept_mask[None, :])
    cotangent = exchange(spread, "expert").reshape(keys, rows)
    state_grad, pieces = call(
        gradients,
        [shape(width, rows), shape(blocks, width, keys // blocks)],
        cotangent,
        state,
        key_value_weight,
    )
    key_value_grad = lax.psum_scatter(pieces, "dp", scatter_dimension=0, tiled=True)[0].astype(f32)
    all_grads = lax.all_gather(state_grad, "dp", axis=0)
    landed = exchange(call(dispatch_grad, slots, gathered, all_grads), "expert")
    down_grad = call(down_gradient, shape(*down_weight.shape[1:]), hidden, landed)
    return (down_grad[None], key_value_grad)


def solution(mesh):
    placed = (
        P("dp", "expert"),
        P(),
        P("dp", None),
        P("dp", None),
        P("expert", None, "dp"),
        P("expert", None, "dp"),
        P("expert", "dp", None),
        P("expert", None),
        P("dp", "expert"),
        P("dp"),
    )
    return jax.shard_map(
        per_device,
        mesh=mesh,
        in_specs=placed,
        out_specs=(P("expert", "dp", None), P("expert", "dp")),
        check_vma=False,
    )
```

```python
import jax
import jax.numpy as jnp
from jax import lax
from jax.experimental import pallas as pl
from jax.experimental.pallas import tpu as pltpu
from jax.sharding import PartitionSpec as P

f32 = jnp.float32
bf16 = jnp.bfloat16
eps_norm = 1e-06
meta_rows = 16
group = 4


def call(body, outs, *operands, limit=16):
    vmem = pl.BlockSpec(memory_space=pltpu.VMEM)
    single = not isinstance(outs, (list, tuple))
    return pl.pallas_call(
        body,
        out_shape=outs,
        in_specs=[vmem] * len(operands),
        out_specs=vmem if single else [vmem] * len(outs),
        compiler_params=pltpu.CompilerParams(vmem_limit_bytes=limit * 1024 * 1024),
    )(*operands)


def iota(shape, axis):
    return lax.broadcasted_iota(jnp.int32, shape, axis)


def contract(a, b, da, db):
    return lax.dot_general(a, b, (((da,), (db,)), ((), ())), preferred_element_type=f32)


def prepare(tok_ref, routes_ref, prob_ref, out_ref):
    rows, experts = tok_ref.shape[0], 32
    out_ref[0:rows, :] = tok_ref[...]
    routes = routes_ref[...].astype(f32)
    first, second = routes[0:1, :], routes[1:2, :]
    names = iota((experts, rows), 0).astype(f32)
    is_first, is_second = names == first, names == second
    named = jnp.where(is_first | is_second, 1.0, 0.0).astype(bf16)
    earlier = jnp.where(iota((rows, rows), 0) < iota((rows, rows), 1), 1.0, 0.0).astype(bf16)
    before = jnp.dot(named, earlier, preferred_element_type=f32)
    slot_first = jnp.sum(jnp.where(is_first, before, 0.0), axis=0, keepdims=True)
    slot_second = jnp.sum(jnp.where(is_second, before, 0.0), axis=0, keepdims=True)
    row = iota((meta_rows, rows), 0)
    meta = jnp.where(
        row == 0,
        first,
        jnp.where(
            row == 1,
            second,
            jnp.where(
                row == 2,
                slot_first,
                jnp.where(
                    row == 3,
                    slot_second,
                    jnp.where(row == 4, prob_ref[0:1, :], jnp.where(row == 5, prob_ref[1:2, :], 0.0)),
                ),
            ),
        ),
    )
    out_ref[rows : rows + meta_rows, :] = meta.astype(bf16)


def selection(meta, inner, capacity, weighted):
    tall = group * capacity
    at = [
        (meta[k : k + 1] * tall + inner * capacity + meta[2 + k : 3 + k]).astype(jnp.int32)
        for k in (0, 1)
    ]
    slots = iota((32 * tall, meta.shape[1]), 0)
    if weighted:
        picked = jnp.where(slots == at[0], meta[4:5], jnp.where(slots == at[1], meta[5:6], 0.0))
    else:
        picked = jnp.where((slots == at[0]) | (slots == at[1]), 1.0, 0.0)
    return picked.astype(bf16)


def block_meta(gathered_ref, block, rows):
    return gathered_ref[block, rows : rows + meta_rows, :].astype(f32)


def dispatch(gathered_ref, out_ref):
    blocks, rows = gathered_ref.shape[0], gathered_ref.shape[1] - meta_rows
    capacity = out_ref.shape[1] // blocks
    tall = group * capacity
    for g in range(blocks // group):
        total = 0.0
        for inner in range(group):
            block = g * group + inner
            chosen = selection(block_meta(gathered_ref, block, rows), inner, capacity, False)
            total = total + jnp.dot(
                chosen, gathered_ref[block, 0:rows, :], preferred_element_type=f32
            )
        for e in range(out_ref.shape[0]):
            out_ref[e, g * tall : (g + 1) * tall, :] = total[e * tall : (e + 1) * tall].astype(bf16)


def dispatch_grad(gathered_ref, grad_ref, out_ref):
    blocks, rows = gathered_ref.shape[0], gathered_ref.shape[1] - meta_rows
    capacity = out_ref.shape[1] // blocks
    tall = group * capacity
    for g in range(blocks // group):
        total = 0.0
        for inner in range(group):
            block = g * group + inner
            chosen = selection(block_meta(gathered_ref, block, rows), inner, capacity, True)
            total = total + contract(chosen, grad_ref[block], 1, 1)
        for e in range(out_ref.shape[0]):
            out_ref[e, g * tall : (g + 1) * tall, :] = total[e * tall : (e + 1) * tall].astype(bf16)


def expert(rows_ref, gain_ref, gate_ref, up_ref, down_ref, out_ref, hidden_ref):
    parts, width = rows_ref.shape[0], rows_ref.shape[2]
    values = jnp.concatenate([rows_ref[p] for p in range(parts)], axis=1).astype(f32)
    mean_sq = jnp.sum(values * values, axis=1, keepdims=True) / (parts * width)
    normed = (values * lax.rsqrt(mean_sq + eps_norm) * gain_ref[...]).astype(bf16)
    gate_val = jnp.dot(normed, gate_ref[...], preferred_element_type=f32)
    up_val = jnp.dot(normed, up_ref[...], preferred_element_type=f32)
    hidden = (gate_val / (1.0 + jnp.exp(-gate_val)) * up_val).astype(bf16)
    hidden_ref[...] = hidden
    product = jnp.dot(hidden, down_ref[...], preferred_element_type=f32)
    for p in range(parts):
        out_ref[p] = product[:, p * width : (p + 1) * width].astype(bf16)


def combine(gathered_ref, back_ref, out_ref):
    blocks, rows = gathered_ref.shape[0], gathered_ref.shape[1] - meta_rows
    capacity = back_ref.shape[1] // blocks
    tall = group * capacity
    for g in range(blocks // group):
        back = jnp.concatenate(
            [back_ref[e, g * tall : (g + 1) * tall, :].astype(f32) for e in range(back_ref.shape[0])],
            axis=0,
        )
        back = back.T.astype(bf16)
        for inner in range(group):
            block = g * group + inner
            chosen = selection(block_meta(gathered_ref, block, rows), inner, capacity, True)
            out_ref[block] = jnp.dot(back, chosen, preferred_element_type=f32).astype(bf16)


def project(pieces_ref, tok_ref, weight_ref, state_ref, out_ref):
    total = tok_ref[...].astype(f32).T
    for p in range(pieces_ref.shape[0]):
        total = total + pieces_ref[p].astype(f32)
    state = total.astype(bf16)
    state_ref[...] = state
    out_ref[...] = contract(weight_ref[...], state, 0, 0).astype(bf16)


def form_cotangent(pieces_ref, target_ref, mask_ref, out_ref):
    total = pieces_ref[0].astype(f32)
    for p in range(1, pieces_ref.shape[0]):
        total = total + pieces_ref[p].astype(f32)
    target = target_ref[...].astype(f32)
    scaled = mask_ref[...].astype(f32) * (total - target) * target.shape[1] ** (-0.5)
    scaled = scaled.astype(bf16)
    for p in range(out_ref.shape[0]):
        out_ref[p] = scaled


def gradients(cot_ref, state_ref, weight_ref, state_grad_ref, pieces_ref):
    state_grad_ref[...] = jnp.dot(
        weight_ref[...], cot_ref[...], preferred_element_type=f32
    ).astype(bf16)
    state = state_ref[...]
    width = cot_ref.shape[0] // pieces_ref.shape[0]
    for p in range(pieces_ref.shape[0]):
        pieces_ref[p] = contract(state, cot_ref[p * width : (p + 1) * width, :], 1, 1).astype(bf16)


def down_gradient(hidden_ref, rows_ref, out_ref):
    hidden = hidden_ref[...].astype(f32).T.astype(bf16)
    width = rows_ref.shape[2]
    for p in range(rows_ref.shape[0]):
        out_ref[:, p * width : (p + 1) * width] = jnp.dot(
            hidden, rows_ref[p], preferred_element_type=f32
        ).astype(bf16)


def per_device(
    tokens,
    norm_gain,
    routes,
    route_prob,
    gate_weight,
    up_weight,
    down_weight,
    key_value_weight,
    key_value_target,
    concept_mask,
):
    rows, width = tokens.shape
    experts = lax.axis_size("expert")
    blocks = lax.axis_size("dp")
    capacity = 5 * rows * routes.shape[1] // (4 * experts)
    keys = key_value_weight.shape[1]

    def shape(*dims, dtype=bf16):
        return jax.ShapeDtypeStruct(dims, dtype)

    def exchange(value, axis):
        return lax.all_to_all(value, axis, split_axis=0, concat_axis=0, tiled=True)

    packed = call(prepare, shape(rows + meta_rows, width), tokens, routes.T, route_prob.T)
    gathered = lax.all_gather(packed, "dp", axis=0)
    slots = shape(experts, blocks * capacity, width)
    arrived = exchange(call(dispatch, slots, gathered), "expert")
    out_rows, hidden = call(
        expert,
        [slots, shape(blocks * capacity, gate_weight.shape[2])],
        arrived,
        norm_gain[None, :],
        gate_weight[0],
        up_weight[0],
        down_weight[0],
        limit=24,
    )
    returned = exchange(out_rows, "expert")
    mixed = exchange(call(combine, shape(blocks, width, rows), gathered, returned), "dp")
    state, proj = call(
        project, [shape(width, rows), shape(keys, rows)], mixed, tokens, key_value_weight
    )
    proj = exchange(proj.reshape(experts, keys // experts, rows), "expert")
    spread = call(
        form_cotangent, shape(*proj.shape), proj, key_value_target.T, concept_mask[None, :]
    )
    cotangent = exchange(spread, "expert").reshape(keys, rows)
    state_grad, pieces = call(
        gradients,
        [shape(width, rows), shape(blocks, width, keys // blocks)],
        cotangent,
        state,
        key_value_weight,
    )
    key_value_grad = lax.psum_scatter(pieces, "dp", scatter_dimension=0, tiled=True)[0].astype(f32)
    all_grads = lax.all_gather(state_grad, "dp", axis=0)
    landed = exchange(call(dispatch_grad, slots, gathered, all_grads), "expert")
    down_grad = call(down_gradient, shape(*down_weight.shape[1:]), hidden, landed)
    return (down_grad[None], key_value_grad)


def solution(mesh):
    placed = (
        P("dp", "expert"),
        P(),
        P("dp", None),
        P("dp", None),
        P("expert", None, "dp"),
        P("expert", None, "dp"),
        P("expert", "dp", None),
        P("expert", None),
        P("dp", "expert"),
        P("dp"),
    )
    return jax.shard_map(
        per_device,
        mesh=mesh,
        in_specs=placed,
        out_specs=(P("expert", "dp", None), P("expert", "dp")),
        check_vma=False,
    )
```

```python
import jax
import jax.numpy as jnp
from jax import lax
from jax.experimental import pallas as pl
from jax.experimental.pallas import tpu as pltpu
from jax.sharding import Mesh
from jax.sharding import PartitionSpec as P

f32 = jnp.float32
bf16 = jnp.bfloat16
eps_norm = 1e-06
meta_rows = 16
group = 4


def call(body, outs, *operands, limit=16):
    vmem = pl.BlockSpec(memory_space=pltpu.VMEM)
    single = not isinstance(outs, (list, tuple))
    return pl.pallas_call(
        body,
        out_shape=outs,
        in_specs=[vmem] * len(operands),
        out_specs=vmem if single else [vmem] * len(outs),
        compiler_params=pltpu.CompilerParams(vmem_limit_bytes=limit * 1024 * 1024),
    )(*operands)


def iota(shape, axis):
    return lax.broadcasted_iota(jnp.int32, shape, axis)


def contract(a, b, da, db):
    return lax.dot_general(a, b, (((da,), (db,)), ((), ())), preferred_element_type=f32)


def prepare(tok_ref, routes_ref, prob_ref, out_ref):
    rows, experts = tok_ref.shape[0], 32
    routes = routes_ref[...].astype(f32)
    first, second = routes[0:1, :], routes[1:2, :]
    names = iota((experts, rows), 0).astype(f32)
    is_first, is_second = names == first, names == second
    named = jnp.where(is_first | is_second, 1.0, 0.0).astype(bf16)
    earlier = jnp.where(iota((rows, rows), 0) < iota((rows, rows), 1), 1.0, 0.0).astype(bf16)
    before = jnp.dot(named, earlier, preferred_element_type=f32)
    slot_first = jnp.sum(jnp.where(is_first, before, 0.0), axis=0, keepdims=True)
    slot_second = jnp.sum(jnp.where(is_second, before, 0.0), axis=0, keepdims=True)
    row = iota((meta_rows, rows), 0)
    meta = jnp.where(
        row == 0,
        first,
        jnp.where(
            row == 1,
            second,
            jnp.where(
                row == 2,
                slot_first,
                jnp.where(
                    row == 3,
                    slot_second,
                    jnp.where(row == 4, prob_ref[0:1, :], jnp.where(row == 5, prob_ref[1:2, :], 0.0)),
                ),
            ),
        ),
    )
    meta = meta.astype(bf16)
    for copy in range(out_ref.shape[0]):
        out_ref[copy, 0:rows, :] = tok_ref[...]
        out_ref[copy, rows : rows + meta_rows, :] = meta


def selection(meta, inner, capacity, weighted):
    tall = group * capacity
    at = [
        (meta[k : k + 1] * tall + inner * capacity + meta[2 + k : 3 + k]).astype(jnp.int32)
        for k in (0, 1)
    ]
    slots = iota((32 * tall, meta.shape[1]), 0)
    if weighted:
        picked = jnp.where(slots == at[0], meta[4:5], jnp.where(slots == at[1], meta[5:6], 0.0))
    else:
        picked = jnp.where((slots == at[0]) | (slots == at[1]), 1.0, 0.0)
    return picked.astype(bf16)


def block_meta(gathered_ref, block, rows):
    return gathered_ref[block, rows : rows + meta_rows, :].astype(f32)


def dispatch(gathered_ref, out_ref):
    blocks, rows = gathered_ref.shape[0], gathered_ref.shape[1] - meta_rows
    capacity = out_ref.shape[2] // blocks
    tall = group * capacity
    for g in range(blocks // group):
        total = 0.0
        for inner in range(group):
            block = g * group + inner
            chosen = selection(block_meta(gathered_ref, block, rows), inner, capacity, False)
            total = total + jnp.dot(
                chosen, gathered_ref[block, 0:rows, :], preferred_element_type=f32
            )
        total = total.astype(bf16)
        for e in range(out_ref.shape[1]):
            for pair in range(out_ref.shape[0]):
                out_ref[pair, e, g * tall : (g + 1) * tall, :] = total[e * tall : (e + 1) * tall]


def dispatch_grad(gathered_ref, grad_ref, out_ref):
    blocks, rows = gathered_ref.shape[0], gathered_ref.shape[1] - meta_rows
    capacity = out_ref.shape[2] // blocks
    tall = group * capacity
    for g in range(blocks // group):
        total = 0.0
        for inner in range(group):
            block = g * group + inner
            chosen = selection(block_meta(gathered_ref, block, rows), inner, capacity, True)
            total = total + contract(chosen, grad_ref[block], 1, 1)
        total = total.astype(bf16)
        for e in range(out_ref.shape[1]):
            for pair in range(out_ref.shape[0]):
                out_ref[pair, e, g * tall : (g + 1) * tall, :] = total[e * tall : (e + 1) * tall]


def expert(rows_ref, gain_ref, gate_ref, up_ref, down_ref, out_ref, hidden_ref):
    pairs, parts, half, width = rows_ref.shape
    values = jnp.concatenate(
        [
            jnp.concatenate([rows_ref[h, p] for p in range(parts)], axis=1)
            for h in range(pairs)
        ],
        axis=0,
    ).astype(f32)
    mean_sq = jnp.sum(values * values, axis=1, keepdims=True) / (parts * width)
    normed = (values * lax.rsqrt(mean_sq + eps_norm) * gain_ref[...]).astype(bf16)
    gate_val = jnp.dot(normed, gate_ref[...], preferred_element_type=f32)
    up_val = jnp.dot(normed, up_ref[...], preferred_element_type=f32)
    hidden = (gate_val / (1.0 + jnp.exp(-gate_val)) * up_val).astype(bf16)
    hidden_ref[...] = hidden
    product = jnp.dot(hidden, down_ref[...], preferred_element_type=f32)
    for h in range(pairs):
        for p in range(parts):
            out_ref[h, p] = product[
                h * half : (h + 1) * half, p * width : (p + 1) * width
            ].astype(bf16)


def combine(gathered_ref, back_ref, out_ref):
    blocks, rows = gathered_ref.shape[0], gathered_ref.shape[1] - meta_rows
    capacity = back_ref.shape[2] // blocks
    tall = group * capacity
    for g in range(blocks // group):
        back = jnp.concatenate(
            [
                sum(
                    back_ref[pair, e, g * tall : (g + 1) * tall, :].astype(f32)
                    for pair in range(back_ref.shape[0])
                )
                for e in range(back_ref.shape[1])
            ],
            axis=0,
        )
        back = back.T.astype(bf16)
        for inner in range(group):
            block = g * group + inner
            chosen = selection(block_meta(gathered_ref, block, rows), inner, capacity, True)
            out_ref[block] = jnp.dot(back, chosen, preferred_element_type=f32).astype(bf16)


def project(pieces_ref, tok_ref, weight_ref, state_ref, out_ref):
    total = tok_ref[...].astype(f32).T
    for p in range(pieces_ref.shape[0]):
        total = total + pieces_ref[p].astype(f32)
    state = total.astype(bf16)
    state_ref[...] = state
    out_ref[...] = contract(weight_ref[...], state, 0, 0).astype(bf16)


def form_cotangent(pieces_ref, target_ref, mask_ref, out_ref):
    total = pieces_ref[0].astype(f32)
    for p in range(1, pieces_ref.shape[0]):
        total = total + pieces_ref[p].astype(f32)
    target = target_ref[...].astype(f32)
    scaled = mask_ref[...].astype(f32) * (total - target) * target.shape[1] ** (-0.5)
    scaled = scaled.astype(bf16)
    for p in range(out_ref.shape[0]):
        out_ref[p] = scaled


def gradients(cot_ref, state_ref, weight_ref, state_grad_ref, pieces_ref):
    state_grad = jnp.dot(
        weight_ref[...], cot_ref[...], preferred_element_type=f32
    ).astype(bf16)
    for copy in range(state_grad_ref.shape[0]):
        state_grad_ref[copy] = state_grad
    state = state_ref[...]
    width = cot_ref.shape[0] // pieces_ref.shape[0]
    for p in range(pieces_ref.shape[0]):
        pieces_ref[p] = contract(state, cot_ref[p * width : (p + 1) * width, :], 1, 1).astype(bf16)


def down_gradient(hidden_ref, rows_ref, out_ref):
    hidden = hidden_ref[...].astype(f32).T.astype(bf16)
    pairs, parts, half, width = rows_ref.shape
    for p in range(parts):
        rows = jnp.concatenate([rows_ref[h, p] for h in range(pairs)], axis=0)
        out_ref[:, p * width : (p + 1) * width] = jnp.dot(
            hidden, rows, preferred_element_type=f32
        ).astype(bf16)


def per_device(
    tokens,
    norm_gain,
    routes,
    route_prob,
    gate_weight,
    up_weight,
    down_weight,
    key_value_weight,
    key_value_target,
    concept_mask,
):
    rows, width = tokens.shape
    experts = lax.axis_size("expert")
    far, near = lax.axis_size("far"), lax.axis_size("near")
    blocks = far * near
    capacity = 5 * rows * routes.shape[1] // (4 * experts)
    keys = key_value_weight.shape[1]

    def shape(*dims, dtype=bf16):
        return jax.ShapeDtypeStruct(dims, dtype)

    def exchange(value, axis):
        return lax.all_to_all(value, axis, split_axis=0, concat_axis=0, tiled=True)

    packed = call(
        prepare, shape(far, rows + meta_rows, width), tokens, routes.T, route_prob.T
    )
    gathered = exchange(packed, "far")
    slots = shape(near, experts, far * capacity, width)
    spots = (near * experts, far * capacity, width)

    def route(value):
        return exchange(value.reshape(spots), ("near", "expert")).reshape(slots.shape)

    arrived = route(call(dispatch, slots, gathered))
    out_rows, hidden = call(
        expert,
        [slots, shape(blocks * capacity, gate_weight.shape[2])],
        arrived,
        norm_gain[None, :],
        gate_weight[0],
        up_weight[0],
        down_weight[0],
        limit=24,
    )
    returned = route(out_rows)
    mixed = exchange(call(combine, shape(far, width, rows), gathered, returned), "far")
    state, proj = call(
        project, [shape(width, rows), shape(keys, rows)], mixed, tokens, key_value_weight
    )
    proj = exchange(proj.reshape(experts, keys // experts, rows), "expert")
    spread = call(
        form_cotangent, shape(*proj.shape), proj, key_value_target.T, concept_mask[None, :]
    )
    cotangent = exchange(spread, "expert").reshape(keys, rows)
    state_grad, pieces = call(
        gradients,
        [shape(far, width, rows), shape(blocks, width, keys // blocks)],
        cotangent,
        state,
        key_value_weight,
    )
    key_value_grad = lax.psum_scatter(
        pieces, ("far", "near"), scatter_dimension=0, tiled=True
    )[0].astype(f32)
    all_grads = exchange(state_grad, "far")
    landed = route(call(dispatch_grad, slots, gathered, all_grads))
    down_grad = call(down_gradient, shape(*down_weight.shape[1:]), hidden, landed)
    return (down_grad[None], key_value_grad)


def solution(mesh):
    blocks, experts = mesh.devices.shape
    fine = Mesh(mesh.devices.reshape(blocks // 2, 2, experts), ("far", "near", "expert"))
    dp = ("far", "near")
    placed = (
        P(dp, "expert"),
        P(),
        P(dp, None),
        P(dp, None),
        P("expert", None, dp),
        P("expert", None, dp),
        P("expert", dp, None),
        P("expert", None),
        P(dp, "expert"),
        P(dp),
    )
    return jax.shard_map(
        per_device,
        mesh=fine,
        in_specs=placed,
        out_specs=(P("expert", dp, None), P("expert", dp)),
        check_vma=False,
    )
```

```python
import jax
import jax.numpy as jnp
from jax import lax
from jax.experimental import pallas as pl
from jax.experimental.pallas import tpu as pltpu
from jax.sharding import Mesh
from jax.sharding import PartitionSpec as P

f32 = jnp.float32
bf16 = jnp.bfloat16
eps_norm = 1e-06
meta_rows = 16
group = 4


def call(body, outs, *operands, limit=16, cost=None):
    vmem = pl.BlockSpec(memory_space=pltpu.VMEM)
    single = not isinstance(outs, (list, tuple))
    return pl.pallas_call(
        body,
        out_shape=outs,
        in_specs=[vmem] * len(operands),
        out_specs=vmem if single else [vmem] * len(outs),
        cost_estimate=cost,
        compiler_params=pltpu.CompilerParams(vmem_limit_bytes=limit * 1024 * 1024),
    )(*operands)


def iota(shape, axis):
    return lax.broadcasted_iota(jnp.int32, shape, axis)


def contract(a, b, da, db):
    return lax.dot_general(a, b, (((da,), (db,)), ((), ())), preferred_element_type=f32)


def prepare(tok_ref, routes_ref, prob_ref, out_ref):
    rows, experts = tok_ref.shape[0], 32
    routes = routes_ref[...].astype(f32)
    first, second = routes[0:1, :], routes[1:2, :]
    names = iota((experts, rows), 0).astype(f32)
    is_first, is_second = names == first, names == second
    named = jnp.where(is_first | is_second, 1.0, 0.0).astype(bf16)
    earlier = jnp.where(iota((rows, rows), 0) < iota((rows, rows), 1), 1.0, 0.0).astype(bf16)
    before = jnp.dot(named, earlier, preferred_element_type=f32)
    slot_first = jnp.sum(jnp.where(is_first, before, 0.0), axis=0, keepdims=True)
    slot_second = jnp.sum(jnp.where(is_second, before, 0.0), axis=0, keepdims=True)
    row = iota((meta_rows, rows), 0)
    meta = jnp.where(
        row == 0,
        first,
        jnp.where(
            row == 1,
            second,
            jnp.where(
                row == 2,
                slot_first,
                jnp.where(
                    row == 3,
                    slot_second,
                    jnp.where(row == 4, prob_ref[0:1, :], jnp.where(row == 5, prob_ref[1:2, :], 0.0)),
                ),
            ),
        ),
    )
    meta = meta.astype(bf16)
    for copy in range(out_ref.shape[0]):
        out_ref[copy, 0:rows, :] = tok_ref[...]
        out_ref[copy, rows : rows + meta_rows, :] = meta


def selection(meta, inner, capacity, weighted):
    tall = group * capacity
    at = [
        (meta[k : k + 1] * tall + inner * capacity + meta[2 + k : 3 + k]).astype(jnp.int32)
        for k in (0, 1)
    ]
    slots = iota((32 * tall, meta.shape[1]), 0)
    if weighted:
        picked = jnp.where(slots == at[0], meta[4:5], jnp.where(slots == at[1], meta[5:6], 0.0))
    else:
        picked = jnp.where((slots == at[0]) | (slots == at[1]), 1.0, 0.0)
    return picked.astype(bf16)


def block_meta(gathered_ref, block, rows):
    return gathered_ref[block, rows : rows + meta_rows, :].astype(f32)


def dispatch(gathered_ref, out_ref):
    blocks, rows = gathered_ref.shape[0], gathered_ref.shape[1] - meta_rows
    capacity = out_ref.shape[2] // blocks
    tall = group * capacity
    for g in range(blocks // group):
        total = 0.0
        for inner in range(group):
            block = g * group + inner
            chosen = selection(block_meta(gathered_ref, block, rows), inner, capacity, False)
            total = total + jnp.dot(
                chosen, gathered_ref[block, 0:rows, :], preferred_element_type=f32
            )
        total = total.astype(bf16)
        for e in range(out_ref.shape[1]):
            for pair in range(out_ref.shape[0]):
                out_ref[pair, e, g * tall : (g + 1) * tall, :] = total[e * tall : (e + 1) * tall]


def dispatch_grad(gathered_ref, grad_ref, out_ref):
    blocks, rows = gathered_ref.shape[0], gathered_ref.shape[1] - meta_rows
    capacity = out_ref.shape[2] // blocks
    tall = group * capacity
    for g in range(blocks // group):
        total = 0.0
        for inner in range(group):
            block = g * group + inner
            chosen = selection(block_meta(gathered_ref, block, rows), inner, capacity, True)
            total = total + contract(chosen, grad_ref[block], 1, 1)
        total = total.astype(bf16)
        for e in range(out_ref.shape[1]):
            for pair in range(out_ref.shape[0]):
                out_ref[pair, e, g * tall : (g + 1) * tall, :] = total[e * tall : (e + 1) * tall]


def expert(rows_ref, gain_ref, gate_ref, up_ref, down_ref, out_ref, hidden_ref):
    pairs, parts, half, width = rows_ref.shape
    values = jnp.concatenate(
        [
            jnp.concatenate([rows_ref[h, p] for p in range(parts)], axis=1)
            for h in range(pairs)
        ],
        axis=0,
    ).astype(f32)
    mean_sq = jnp.sum(values * values, axis=1, keepdims=True) / (parts * width)
    normed = (values * lax.rsqrt(mean_sq + eps_norm) * gain_ref[...]).astype(bf16)
    gate_val = jnp.dot(normed, gate_ref[...], preferred_element_type=f32)
    up_val = jnp.dot(normed, up_ref[...], preferred_element_type=f32)
    hidden = (gate_val / (1.0 + jnp.exp(-gate_val)) * up_val).astype(bf16)
    hidden_ref[...] = hidden
    product = jnp.dot(hidden, down_ref[...], preferred_element_type=f32)
    for h in range(pairs):
        for p in range(parts):
            out_ref[h, p] = product[
                h * half : (h + 1) * half, p * width : (p + 1) * width
            ].astype(bf16)


def combine(gathered_ref, back_ref, out_ref):
    blocks, rows = gathered_ref.shape[0], gathered_ref.shape[1] - meta_rows
    capacity = back_ref.shape[2] // blocks
    tall = group * capacity
    for g in range(blocks // group):
        back = jnp.concatenate(
            [
                sum(
                    back_ref[pair, e, g * tall : (g + 1) * tall, :].astype(f32)
                    for pair in range(back_ref.shape[0])
                )
                for e in range(back_ref.shape[1])
            ],
            axis=0,
        )
        back = back.T.astype(bf16)
        for inner in range(group):
            block = g * group + inner
            chosen = selection(block_meta(gathered_ref, block, rows), inner, capacity, True)
            out_ref[block] = jnp.dot(back, chosen, preferred_element_type=f32).astype(bf16)


def project(pieces_ref, tok_ref, weight_ref, state_ref, out_ref):
    total = tok_ref[...].astype(f32).T
    for p in range(pieces_ref.shape[0]):
        total = total + pieces_ref[p].astype(f32)
    state = total.astype(bf16)
    state_ref[...] = state
    out_ref[...] = contract(weight_ref[...], state, 0, 0).astype(bf16)


def form_cotangent(pieces_ref, target_ref, mask_ref, out_ref):
    total = pieces_ref[0].astype(f32)
    for p in range(1, pieces_ref.shape[0]):
        total = total + pieces_ref[p].astype(f32)
    target = target_ref[...].astype(f32)
    scaled = mask_ref[...].astype(f32) * (total - target) * target.shape[1] ** (-0.5)
    scaled = scaled.astype(bf16)
    for p in range(out_ref.shape[0]):
        out_ref[p] = scaled


def gradients(cot_ref, state_ref, weight_ref, state_grad_ref, pieces_ref):
    state_grad = jnp.dot(
        weight_ref[...], cot_ref[...], preferred_element_type=f32
    ).astype(bf16)
    for copy in range(state_grad_ref.shape[0]):
        state_grad_ref[copy] = state_grad
    state = state_ref[...]
    width = cot_ref.shape[0] // pieces_ref.shape[0]
    for p in range(pieces_ref.shape[0]):
        pieces_ref[p] = contract(state, cot_ref[p * width : (p + 1) * width, :], 1, 1).astype(bf16)


def down_gradient(hidden_ref, rows_ref, out_ref):
    hidden = hidden_ref[...].astype(f32).T.astype(bf16)
    pairs, parts, half, width = rows_ref.shape
    for p in range(parts):
        rows = jnp.concatenate([rows_ref[h, p] for h in range(pairs)], axis=0)
        out_ref[:, p * width : (p + 1) * width] = jnp.dot(
            hidden, rows, preferred_element_type=f32
        ).astype(bf16)


def widen(piece_ref, out_ref):
    out_ref[...] = piece_ref[...].astype(f32)


def per_device(
    tokens,
    norm_gain,
    routes,
    route_prob,
    gate_weight,
    up_weight,
    down_weight,
    key_value_weight,
    key_value_target,
    concept_mask,
):
    rows, width = tokens.shape
    experts = lax.axis_size("expert")
    far, near = lax.axis_size("far"), lax.axis_size("near")
    blocks = far * near
    capacity = 5 * rows * routes.shape[1] // (4 * experts)
    keys = key_value_weight.shape[1]

    def shape(*dims, dtype=bf16):
        return jax.ShapeDtypeStruct(dims, dtype)

    def exchange(value, axis):
        return lax.all_to_all(value, axis, split_axis=0, concat_axis=0, tiled=True)

    packed = call(
        prepare, shape(far, rows + meta_rows, width), tokens, routes.T, route_prob.T
    )
    gathered = exchange(packed, "far")
    slots = shape(near, experts, far * capacity, width)
    spots = (near * experts, far * capacity, width)

    def route(value):
        return exchange(value.reshape(spots), ("near", "expert")).reshape(slots.shape)

    arrived = route(call(dispatch, slots, gathered))
    out_rows, hidden = call(
        expert,
        [slots, shape(blocks * capacity, gate_weight.shape[2])],
        arrived,
        norm_gain[None, :],
        gate_weight[0],
        up_weight[0],
        down_weight[0],
        limit=24,
    )
    returned = route(out_rows)
    mixed = exchange(call(combine, shape(far, width, rows), gathered, returned), "far")
    state, proj = call(
        project, [shape(width, rows), shape(keys, rows)], mixed, tokens, key_value_weight
    )
    proj = exchange(proj.reshape(experts, keys // experts, rows), "expert")
    spread = call(
        form_cotangent, shape(*proj.shape), proj, key_value_target.T, concept_mask[None, :]
    )
    cotangent = exchange(spread, "expert").reshape(keys, rows)
    state_grad, pieces = call(
        gradients,
        [shape(far, width, rows), shape(blocks, width, keys // blocks)],
        cotangent,
        state,
        key_value_weight,
    )
    key_value_grad = lax.psum_scatter(
        pieces, ("far", "near"), scatter_dimension=0, tiled=True
    )[0]
    key_value_grad = call(
        widen,
        shape(width, keys // blocks, dtype=f32),
        key_value_grad,
        cost=pl.CostEstimate(flops=10**12, bytes_accessed=1 << 17, transcendentals=0),
    )
    all_grads = exchange(state_grad, "far")
    landed = route(call(dispatch_grad, slots, gathered, all_grads))
    landed, key_value_grad = lax.optimization_barrier((landed, key_value_grad))
    down_grad = call(down_gradient, shape(*down_weight.shape[1:]), hidden, landed)
    return (down_grad[None], key_value_grad)


def solution(mesh):
    blocks, experts = mesh.devices.shape
    fine = Mesh(mesh.devices.reshape(blocks // 2, 2, experts), ("far", "near", "expert"))
    dp = ("far", "near")
    placed = (
        P(dp, "expert"),
        P(),
        P(dp, None),
        P(dp, None),
        P("expert", None, dp),
        P("expert", None, dp),
        P("expert", dp, None),
        P("expert", None),
        P(dp, "expert"),
        P(dp),
    )
    return jax.shard_map(
        per_device,
        mesh=fine,
        in_specs=placed,
        out_specs=(P("expert", dp, None), P("expert", dp)),
        check_vma=False,
    )
```

```python
import jax
import jax.numpy as jnp
from jax import lax
from jax.experimental import pallas as pl
from jax.experimental.pallas import tpu as pltpu
from jax.sharding import Mesh
from jax.sharding import PartitionSpec as P

f32 = jnp.float32
bf16 = jnp.bfloat16
eps_norm = 1e-06
meta_rows = 16
group = 4


def call(body, outs, *operands, limit=16, scalars=0):
    vmem = pl.BlockSpec(memory_space=pltpu.VMEM)
    smem = pl.BlockSpec(memory_space=pltpu.SMEM)
    single = not isinstance(outs, (list, tuple))
    return pl.pallas_call(
        body,
        out_shape=outs,
        in_specs=[smem] * scalars + [vmem] * (len(operands) - scalars),
        out_specs=vmem if single else [vmem] * len(outs),
        compiler_params=pltpu.CompilerParams(vmem_limit_bytes=limit * 1024 * 1024),
    )(*operands)


def iota(shape, axis):
    return lax.broadcasted_iota(jnp.int32, shape, axis)


def contract(a, b, da, db):
    return lax.dot_general(a, b, (((da,), (db,)), ((), ())), preferred_element_type=f32)


def prepare(tok_ref, routes_ref, prob_ref, out_ref):
    rows, experts = tok_ref.shape[0], 32
    routes = routes_ref[...].astype(f32)
    first, second = routes[0:1, :], routes[1:2, :]
    names = iota((experts, rows), 0).astype(f32)
    is_first, is_second = names == first, names == second
    named = jnp.where(is_first | is_second, 1.0, 0.0).astype(bf16)
    earlier = jnp.where(iota((rows, rows), 0) < iota((rows, rows), 1), 1.0, 0.0).astype(bf16)
    before = jnp.dot(named, earlier, preferred_element_type=f32)
    slot_first = jnp.sum(jnp.where(is_first, before, 0.0), axis=0, keepdims=True)
    slot_second = jnp.sum(jnp.where(is_second, before, 0.0), axis=0, keepdims=True)
    row = iota((meta_rows, rows), 0)
    meta = jnp.where(
        row == 0,
        first,
        jnp.where(
            row == 1,
            second,
            jnp.where(
                row == 2,
                slot_first,
                jnp.where(
                    row == 3,
                    slot_second,
                    jnp.where(row == 4, prob_ref[0:1, :], jnp.where(row == 5, prob_ref[1:2, :], 0.0)),
                ),
            ),
        ),
    )
    meta = meta.astype(bf16)
    for copy in range(out_ref.shape[0]):
        out_ref[copy, 0:rows, :] = tok_ref[...]
        out_ref[copy, rows : rows + meta_rows, :] = meta


def selection(meta, inner, capacity, weighted):
    tall = group * capacity
    at = [
        (meta[k : k + 1] * tall + inner * capacity + meta[2 + k : 3 + k]).astype(jnp.int32)
        for k in (0, 1)
    ]
    slots = iota((32 * tall, meta.shape[1]), 0)
    if weighted:
        picked = jnp.where(slots == at[0], meta[4:5], jnp.where(slots == at[1], meta[5:6], 0.0))
    else:
        picked = jnp.where((slots == at[0]) | (slots == at[1]), 1.0, 0.0)
    return picked.astype(bf16)


def block_meta(gathered_ref, block, rows):
    return gathered_ref[block, rows : rows + meta_rows, :].astype(f32)


def dispatch(gathered_ref, out_ref):
    blocks, rows = gathered_ref.shape[0], gathered_ref.shape[1] - meta_rows
    capacity = out_ref.shape[2] // blocks
    tall = group * capacity
    for g in range(blocks // group):
        total = 0.0
        for inner in range(group):
            block = g * group + inner
            chosen = selection(block_meta(gathered_ref, block, rows), inner, capacity, False)
            total = total + jnp.dot(
                chosen, gathered_ref[block, 0:rows, :], preferred_element_type=f32
            )
        total = total.astype(bf16)
        for e in range(out_ref.shape[1]):
            for pair in range(out_ref.shape[0]):
                out_ref[pair, e, g * tall : (g + 1) * tall, :] = total[e * tall : (e + 1) * tall]


def dispatch_grad(gathered_ref, grad_ref, out_ref):
    blocks, rows = gathered_ref.shape[0], gathered_ref.shape[1] - meta_rows
    capacity = out_ref.shape[2] // blocks
    tall = group * capacity
    for g in range(blocks // group):
        total = 0.0
        for inner in range(group):
            block = g * group + inner
            chosen = selection(block_meta(gathered_ref, block, rows), inner, capacity, True)
            total = total + contract(chosen, grad_ref[block, 0:rows, :], 1, 1)
        total = total.astype(bf16)
        for e in range(out_ref.shape[1]):
            for pair in range(out_ref.shape[0]):
                out_ref[pair, e, g * tall : (g + 1) * tall, :] = total[e * tall : (e + 1) * tall]


def expert(rows_ref, gain_ref, gate_ref, up_ref, down_ref, out_ref, hidden_ref):
    pairs, parts, half, width = rows_ref.shape
    values = jnp.concatenate(
        [
            jnp.concatenate([rows_ref[h, p] for p in range(parts)], axis=1)
            for h in range(pairs)
        ],
        axis=0,
    ).astype(f32)
    mean_sq = jnp.sum(values * values, axis=1, keepdims=True) / (parts * width)
    normed = (values * lax.rsqrt(mean_sq + eps_norm) * gain_ref[...]).astype(bf16)
    gate_val = jnp.dot(normed, gate_ref[...], preferred_element_type=f32)
    up_val = jnp.dot(normed, up_ref[...], preferred_element_type=f32)
    hidden = (gate_val / (1.0 + jnp.exp(-gate_val)) * up_val).astype(bf16)
    hidden_ref[...] = hidden
    product = jnp.dot(hidden, down_ref[...], preferred_element_type=f32)
    for h in range(pairs):
        for p in range(parts):
            out_ref[h, p] = product[
                h * half : (h + 1) * half, p * width : (p + 1) * width
            ].astype(bf16)


def combine(gathered_ref, back_ref, out_ref):
    blocks, rows = gathered_ref.shape[0], gathered_ref.shape[1] - meta_rows
    capacity = back_ref.shape[2] // blocks
    tall = group * capacity
    for g in range(blocks // group):
        back = jnp.concatenate(
            [
                sum(
                    back_ref[pair, e, g * tall : (g + 1) * tall, :].astype(f32)
                    for pair in range(back_ref.shape[0])
                )
                for e in range(back_ref.shape[1])
            ],
            axis=0,
        )
        back = back.T.astype(bf16)
        for inner in range(group):
            block = g * group + inner
            chosen = selection(block_meta(gathered_ref, block, rows), inner, capacity, True)
            out_ref[block] = jnp.dot(back, chosen, preferred_element_type=f32).astype(bf16)


def project(pieces_ref, tok_ref, weight_ref, state_ref, out_ref):
    total = tok_ref[...].astype(f32).T
    for p in range(pieces_ref.shape[0]):
        total = total + pieces_ref[p].astype(f32)
    state = total.astype(bf16)
    state_ref[...] = state
    out_ref[...] = contract(weight_ref[...], state, 0, 0).astype(bf16)


def form_cotangent(pieces_ref, target_ref, mask_ref, out_ref):
    total = pieces_ref[0].astype(f32)
    for p in range(1, pieces_ref.shape[0]):
        total = total + pieces_ref[p].astype(f32)
    target = target_ref[...].astype(f32)
    scaled = mask_ref[...].astype(f32) * (total - target) * target.shape[1] ** (-0.5)
    scaled = scaled.astype(bf16)
    for p in range(out_ref.shape[0]):
        out_ref[p] = scaled


def gradients(cot_ref, state_ref, weight_ref, out_ref):
    width = weight_ref.shape[0]
    state_grad = jnp.dot(
        weight_ref[...], cot_ref[...], preferred_element_type=f32
    ).astype(bf16)
    state = state_ref[...]
    near = out_ref.shape[1] // width - 1
    columns = cot_ref.shape[0] // (out_ref.shape[0] * near)
    for q in range(out_ref.shape[0]):
        out_ref[q, 0:width, :] = state_grad
        for p in range(near):
            at = (q * near + p) * columns
            out_ref[q, (p + 1) * width : (p + 2) * width, :] = contract(
                state, cot_ref[at : at + columns, :], 1, 1
            ).astype(bf16)


def add_parts(parity_ref, parts_ref, mine_ref, other_ref):
    width = mine_ref.shape[0]
    totals = [
        sum(
            parts_ref[q, (p + 1) * width : (p + 2) * width, :].astype(f32)
            for q in range(parts_ref.shape[0])
        )
        for p in (0, 1)
    ]
    even = parity_ref[0] == 0
    mine_ref[...] = jnp.where(even, totals[0], totals[1])
    other_ref[...] = jnp.where(even, totals[1], totals[0])


def down_gradient(hidden_ref, rows_ref, mine_ref, other_ref, out_ref, key_value_ref):
    key_value_ref[...] = mine_ref[...] + other_ref[...]
    hidden = hidden_ref[...].astype(f32).T.astype(bf16)
    pairs, parts, half, width = rows_ref.shape
    for p in range(parts):
        rows = jnp.concatenate([rows_ref[h, p] for h in range(pairs)], axis=0)
        out_ref[:, p * width : (p + 1) * width] = jnp.dot(
            hidden, rows, preferred_element_type=f32
        ).astype(bf16)


def per_device(
    tokens,
    norm_gain,
    routes,
    route_prob,
    gate_weight,
    up_weight,
    down_weight,
    key_value_weight,
    key_value_target,
    concept_mask,
):
    rows, width = tokens.shape
    experts = lax.axis_size("expert")
    far, near = lax.axis_size("far"), lax.axis_size("near")
    blocks = far * near
    capacity = 5 * rows * routes.shape[1] // (4 * experts)
    keys = key_value_weight.shape[1]

    def shape(*dims, dtype=bf16):
        return jax.ShapeDtypeStruct(dims, dtype)

    def exchange(value, axis):
        return lax.all_to_all(value, axis, split_axis=0, concat_axis=0, tiled=True)

    packed = call(
        prepare, shape(far, rows + meta_rows, width), tokens, routes.T, route_prob.T
    )
    gathered = exchange(packed, "far")
    slots = shape(near, experts, far * capacity, width)
    spots = (near * experts, far * capacity, width)

    def route(value):
        return exchange(value.reshape(spots), ("near", "expert")).reshape(slots.shape)

    arrived = route(call(dispatch, slots, gathered))
    out_rows, hidden = call(
        expert,
        [slots, shape(blocks * capacity, gate_weight.shape[2])],
        arrived,
        norm_gain[None, :],
        gate_weight[0],
        up_weight[0],
        down_weight[0],
        limit=24,
    )
    returned = route(out_rows)
    mixed = exchange(call(combine, shape(far, width, rows), gathered, returned), "far")
    state, proj = call(
        project, [shape(width, rows), shape(keys, rows)], mixed, tokens, key_value_weight
    )
    proj = exchange(proj.reshape(experts, keys // experts, rows), "expert")
    spread = call(
        form_cotangent, shape(*proj.shape), proj, key_value_target.T, concept_mask[None, :]
    )
    cotangent = exchange(spread, "expert").reshape(keys, rows)
    sent = call(
        gradients, shape(far, (near + 1) * width, rows), cotangent, state, key_value_weight
    )
    all_grads = exchange(sent, "far")
    part = shape(width, keys // blocks, dtype=f32)
    mine, other = call(
        add_parts,
        [part, part],
        lax.axis_index("near").astype(jnp.int32)[None],
        all_grads,
        scalars=1,
    )
    other = lax.ppermute(other, "near", [(0, 1), (1, 0)])
    landed = route(call(dispatch_grad, slots, gathered, all_grads))
    down_grad, key_value_grad = call(
        down_gradient, [shape(*down_weight.shape[1:]), part], hidden, landed, mine, other
    )
    return (down_grad[None], key_value_grad)


def solution(mesh):
    blocks, experts = mesh.devices.shape
    fine = Mesh(mesh.devices.reshape(blocks // 2, 2, experts), ("far", "near", "expert"))
    dp = ("far", "near")
    placed = (
        P(dp, "expert"),
        P(),
        P(dp, None),
        P(dp, None),
        P("expert", None, dp),
        P("expert", None, dp),
        P("expert", dp, None),
        P("expert", None),
        P(dp, "expert"),
        P(dp),
    )
    return jax.shard_map(
        per_device,
        mesh=fine,
        in_specs=placed,
        out_specs=(P("expert", dp, None), P("expert", dp)),
        check_vma=False,
    )
```

```python
import jax
import jax.numpy as jnp
from jax import lax
from jax.experimental import pallas as pl
from jax.experimental.pallas import tpu as pltpu
from jax.sharding import Mesh
from jax.sharding import PartitionSpec as P

f32 = jnp.float32
bf16 = jnp.bfloat16
eps_norm = 1e-06
meta_rows = 16
half_tile = 32
group = 4


def call(body, outs, *operands, limit=16, cost=None):
    vmem = pl.BlockSpec(memory_space=pltpu.VMEM)
    single = not isinstance(outs, (list, tuple))
    return pl.pallas_call(
        body,
        out_shape=outs,
        in_specs=[vmem] * len(operands),
        out_specs=vmem if single else [vmem] * len(outs),
        cost_estimate=cost,
        compiler_params=pltpu.CompilerParams(vmem_limit_bytes=limit * 1024 * 1024),
    )(*operands)


def iota(shape, axis):
    return lax.broadcasted_iota(jnp.int32, shape, axis)


def contract(a, b, da, db):
    return lax.dot_general(a, b, (((da,), (db,)), ((), ())), preferred_element_type=f32)


def prepare(tok_ref, routes_ref, prob_ref, out_ref):
    rows, experts = tok_ref.shape[0], 32
    routes = routes_ref[...].astype(f32)
    first, second = routes[0:1, :], routes[1:2, :]
    names = iota((experts, rows), 0).astype(f32)
    is_first, is_second = names == first, names == second
    named = jnp.where(is_first | is_second, 1.0, 0.0).astype(bf16)
    earlier = jnp.where(iota((rows, rows), 0) < iota((rows, rows), 1), 1.0, 0.0).astype(bf16)
    before = jnp.dot(named, earlier, preferred_element_type=f32)
    slot_first = jnp.sum(jnp.where(is_first, before, 0.0), axis=0, keepdims=True)
    slot_second = jnp.sum(jnp.where(is_second, before, 0.0), axis=0, keepdims=True)
    row = iota((meta_rows, rows), 0)
    meta = jnp.where(
        row == 0,
        first,
        jnp.where(
            row == 1,
            second,
            jnp.where(
                row == 2,
                slot_first,
                jnp.where(
                    row == 3,
                    slot_second,
                    jnp.where(row == 4, prob_ref[0:1, :], jnp.where(row == 5, prob_ref[1:2, :], 0.0)),
                ),
            ),
        ),
    )
    meta = meta.astype(bf16)
    for copy in range(out_ref.shape[0]):
        out_ref[copy, 0:rows, :] = tok_ref[...]
        out_ref[copy, rows : rows + meta_rows, :] = meta


def selection(meta, inner, capacity, weighted):
    tall = group * capacity
    at = [
        (meta[k : k + 1] * tall + inner * capacity + meta[2 + k : 3 + k]).astype(jnp.int32)
        for k in (0, 1)
    ]
    slots = iota((32 * tall, meta.shape[1]), 0)
    if weighted:
        picked = jnp.where(slots == at[0], meta[4:5], jnp.where(slots == at[1], meta[5:6], 0.0))
    else:
        picked = jnp.where((slots == at[0]) | (slots == at[1]), 1.0, 0.0)
    return picked.astype(bf16)


def block_meta(gathered_ref, block, rows):
    return gathered_ref[block, rows : rows + meta_rows, :].astype(f32)


def dispatch(gathered_ref, out_ref):
    blocks, rows = gathered_ref.shape[0], gathered_ref.shape[1] - meta_rows
    capacity = out_ref.shape[2] // blocks
    tall = group * capacity
    for g in range(blocks // group):
        total = 0.0
        for inner in range(group):
            block = g * group + inner
            chosen = selection(block_meta(gathered_ref, block, rows), inner, capacity, False)
            total = total + jnp.dot(
                chosen, gathered_ref[block, 0:rows, :], preferred_element_type=f32
            )
        total = total.astype(bf16)
        for e in range(out_ref.shape[1]):
            for pair in range(out_ref.shape[0]):
                out_ref[pair, e, g * tall : (g + 1) * tall, :] = total[e * tall : (e + 1) * tall]


def dispatch_grad(gathered_ref, grad_ref, same_ref, cross_ref, out_ref):
    blocks, rows = gathered_ref.shape[0], gathered_ref.shape[1] - meta_rows
    capacity = (out_ref.shape[2] - half_tile) // blocks
    tall = group * capacity
    for g in range(blocks // group):
        total = 0.0
        for inner in range(group):
            block = g * group + inner
            chosen = selection(block_meta(gathered_ref, block, rows), inner, capacity, True)
            total = total + contract(chosen, grad_ref[block], 1, 1)
        total = total.astype(bf16)
        for e in range(out_ref.shape[1]):
            for pair in range(out_ref.shape[0]):
                out_ref[pair, e, g * tall : (g + 1) * tall, :] = total[e * tall : (e + 1) * tall]
    even = lax.axis_index("near") == 0
    same, cross = same_ref[...].astype(f32), cross_ref[...].astype(f32)
    tiles = [
        jnp.where(even, same, cross).astype(bf16),
        jnp.where(even, cross, same).astype(bf16),
    ]
    for pair in range(out_ref.shape[0]):
        for e in range(out_ref.shape[1]):
            out_ref[pair, e, blocks * capacity :, :] = tiles[pair]


def expert(rows_ref, gain_ref, gate_ref, up_ref, down_ref, out_ref, hidden_ref):
    pairs, parts, half, width = rows_ref.shape
    values = jnp.concatenate(
        [
            jnp.concatenate([rows_ref[h, p] for p in range(parts)], axis=1)
            for h in range(pairs)
        ],
        axis=0,
    ).astype(f32)
    mean_sq = jnp.sum(values * values, axis=1, keepdims=True) / (parts * width)
    normed = (values * lax.rsqrt(mean_sq + eps_norm) * gain_ref[...]).astype(bf16)
    gate_val = jnp.dot(normed, gate_ref[...], preferred_element_type=f32)
    up_val = jnp.dot(normed, up_ref[...], preferred_element_type=f32)
    hidden = (gate_val / (1.0 + jnp.exp(-gate_val)) * up_val).astype(bf16)
    hidden_ref[...] = hidden
    product = jnp.dot(hidden, down_ref[...], preferred_element_type=f32)
    for h in range(pairs):
        for p in range(parts):
            out_ref[h, p] = product[
                h * half : (h + 1) * half, p * width : (p + 1) * width
            ].astype(bf16)


def combine(gathered_ref, back_ref, out_ref):
    blocks, rows = gathered_ref.shape[0], gathered_ref.shape[1] - meta_rows
    capacity = back_ref.shape[2] // blocks
    tall = group * capacity
    for g in range(blocks // group):
        back = jnp.concatenate(
            [
                sum(
                    back_ref[pair, e, g * tall : (g + 1) * tall, :].astype(f32)
                    for pair in range(back_ref.shape[0])
                )
                for e in range(back_ref.shape[1])
            ],
            axis=0,
        )
        back = back.T.astype(bf16)
        for inner in range(group):
            block = g * group + inner
            chosen = selection(block_meta(gathered_ref, block, rows), inner, capacity, True)
            out_ref[block] = jnp.dot(back, chosen, preferred_element_type=f32).astype(bf16)


def project(pieces_ref, tok_ref, weight_ref, out_ref, state_ref):
    total = tok_ref[...].astype(f32).T
    for p in range(pieces_ref.shape[0]):
        total = total + pieces_ref[p].astype(f32)
    state = total.astype(bf16)
    state_ref[...] = state.astype(f32)
    out_ref[...] = contract(weight_ref[...], state, 0, 0).astype(bf16)


def form_cotangent(pieces_ref, target_ref, mask_ref, out_ref, same_ref, cross_ref):
    total = pieces_ref[0].astype(f32)
    for p in range(1, pieces_ref.shape[0]):
        total = total + pieces_ref[p].astype(f32)
    target = target_ref[...].astype(f32)
    scaled = mask_ref[...].astype(f32) * (total - target) * target.shape[1] ** (-0.5)
    scaled = scaled.astype(bf16)
    for p in range(out_ref.shape[0]):
        out_ref[p] = scaled
    even = (lax.axis_index("expert") // 2) % 2 == 0
    low, high = scaled[0:half_tile].astype(f32), scaled[half_tile:].astype(f32)
    same_ref[...] = jnp.where(even, low, high).astype(bf16)
    cross_ref[...] = jnp.where(even, high, low).astype(bf16)


def backpropagate(cot_ref, weight_ref, out_ref):
    state_grad = jnp.dot(
        weight_ref[...], cot_ref[...], preferred_element_type=f32
    ).astype(bf16)
    for copy in range(out_ref.shape[0]):
        out_ref[copy] = state_grad


def narrow(state_ref, out_ref):
    out_ref[...] = state_ref[...].astype(bf16)


def down_gradient(hidden_ref, rows_ref, state_ref, out_ref, key_value_ref):
    hidden = hidden_ref[...].astype(f32).T.astype(bf16)
    pairs, parts, tall, width = rows_ref.shape
    half = tall - half_tile
    for p in range(parts):
        rows = jnp.concatenate([rows_ref[h, p, 0:half, :] for h in range(pairs)], axis=0)
        out_ref[:, p * width : (p + 1) * width] = jnp.dot(
            hidden, rows, preferred_element_type=f32
        ).astype(bf16)
    total = 0.0
    for block in range(state_ref.shape[0]):
        cotangent = jnp.concatenate(
            [rows_ref[h, 2 * block + side, half:, :] for side in (0, 1) for h in range(pairs)],
            axis=0,
        )
        total = total + contract(state_ref[block], cotangent, 1, 1)
    key_value_ref[...] = total


def per_device(
    tokens,
    norm_gain,
    routes,
    route_prob,
    gate_weight,
    up_weight,
    down_weight,
    key_value_weight,
    key_value_target,
    concept_mask,
):
    rows, width = tokens.shape
    experts = lax.axis_size("expert")
    far, near = lax.axis_size("far"), lax.axis_size("near")
    blocks = far * near
    capacity = 5 * rows * routes.shape[1] // (4 * experts)
    keys = key_value_weight.shape[1]

    def shape(*dims, dtype=bf16):
        return jax.ShapeDtypeStruct(dims, dtype)

    def exchange(value, axis):
        return lax.all_to_all(value, axis, split_axis=0, concat_axis=0, tiled=True)

    packed = call(
        prepare, shape(far, rows + meta_rows, width), tokens, routes.T, route_prob.T
    )
    gathered = exchange(packed, "far")
    slots = shape(near, experts, far * capacity, width)

    def route(value):
        flat = value.reshape(near * experts, *value.shape[2:])
        return exchange(flat, ("near", "expert")).reshape(value.shape)

    arrived = route(call(dispatch, slots, gathered))
    out_rows, hidden = call(
        expert,
        [slots, shape(blocks * capacity, gate_weight.shape[2])],
        arrived,
        norm_gain[None, :],
        gate_weight[0],
        up_weight[0],
        down_weight[0],
        limit=24,
    )
    returned = route(out_rows)
    mixed = exchange(call(combine, shape(far, width, rows), gathered, returned), "far")
    proj, state = call(
        project,
        [shape(keys, rows), shape(width, rows, dtype=f32)],
        mixed,
        tokens,
        key_value_weight,
    )
    states = lax.all_gather(state, ("far", "near"), axis=0)
    states = call(
        narrow,
        shape(blocks, width, rows),
        states,
        cost=pl.CostEstimate(flops=10**12, bytes_accessed=3 << 19, transcendentals=0),
    )
    proj = exchange(proj.reshape(experts, keys // experts, rows), "expert")
    part = shape(half_tile, rows)
    spread, same, cross = call(
        form_cotangent,
        [shape(*proj.shape), part, part],
        proj,
        key_value_target.T,
        concept_mask[None, :],
    )
    moves = [[], []]
    for block in range(blocks):
        for c in range(experts):
            plane, lane = c // 2, 2 * block + c % 2
            for flip in (0, 1):
                moves[flip].append((block * experts + c, (plane ^ flip) * experts + lane))
    everyone = ("far", "near", "expert")
    same = lax.ppermute(same, everyone, moves[0])
    cross = lax.ppermute(cross, everyone, moves[1])
    cotangent = exchange(spread, "expert").reshape(keys, rows)
    state_grad = call(backpropagate, shape(far, width, rows), cotangent, key_value_weight)
    all_grads = exchange(state_grad, "far")
    tall_slots = shape(near, experts, far * capacity + half_tile, width)
    landed = route(call(dispatch_grad, tall_slots, gathered, all_grads, same, cross))
    landed, states = lax.optimization_barrier((landed, states))
    down_grad, key_value_grad = call(
        down_gradient,
        [shape(*down_weight.shape[1:]), shape(width, keys // blocks, dtype=f32)],
        hidden,
        landed,
        states,
    )
    return (down_grad[None], key_value_grad)


def solution(mesh):
    blocks, experts = mesh.devices.shape
    fine = Mesh(mesh.devices.reshape(blocks // 2, 2, experts), ("far", "near", "expert"))
    dp = ("far", "near")
    placed = (
        P(dp, "expert"),
        P(),
        P(dp, None),
        P(dp, None),
        P("expert", None, dp),
        P("expert", None, dp),
        P("expert", dp, None),
        P("expert", None),
        P(dp, "expert"),
        P(dp),
    )
    return jax.shard_map(
        per_device,
        mesh=fine,
        in_specs=placed,
        out_specs=(P("expert", dp, None), P("expert", dp)),
        check_vma=False,
    )
```

```python
import jax
import jax.numpy as jnp
from jax import lax
from jax.experimental import pallas as pl
from jax.experimental.pallas import tpu as pltpu
from jax.sharding import Mesh
from jax.sharding import PartitionSpec as P

f32 = jnp.float32
bf16 = jnp.bfloat16
eps_norm = 1e-06
meta_rows = 16
group = 4


def call(body, outs, *operands, limit=16):
    vmem = pl.BlockSpec(memory_space=pltpu.VMEM)
    single = not isinstance(outs, (list, tuple))
    return pl.pallas_call(
        body,
        out_shape=outs,
        in_specs=[vmem] * len(operands),
        out_specs=vmem if single else [vmem] * len(outs),
        compiler_params=pltpu.CompilerParams(vmem_limit_bytes=limit * 1024 * 1024),
    )(*operands)


def iota(shape, axis):
    return lax.broadcasted_iota(jnp.int32, shape, axis)


def contract(a, b, da, db):
    return lax.dot_general(a, b, (((da,), (db,)), ((), ())), preferred_element_type=f32)


def prepare(tok_ref, routes_ref, prob_ref, out_ref):
    rows, experts = tok_ref.shape[0], 32
    routes = routes_ref[...].astype(f32)
    first, second = routes[0:1, :], routes[1:2, :]
    names = iota((experts, rows), 0).astype(f32)
    is_first, is_second = names == first, names == second
    named = jnp.where(is_first | is_second, 1.0, 0.0).astype(bf16)
    earlier = jnp.where(iota((rows, rows), 0) < iota((rows, rows), 1), 1.0, 0.0).astype(bf16)
    before = jnp.dot(named, earlier, preferred_element_type=f32)
    slot_first = jnp.sum(jnp.where(is_first, before, 0.0), axis=0, keepdims=True)
    slot_second = jnp.sum(jnp.where(is_second, before, 0.0), axis=0, keepdims=True)
    row = iota((meta_rows, rows), 0)
    meta = jnp.where(
        row == 0,
        first,
        jnp.where(
            row == 1,
            second,
            jnp.where(
                row == 2,
                slot_first,
                jnp.where(
                    row == 3,
                    slot_second,
                    jnp.where(row == 4, prob_ref[0:1, :], jnp.where(row == 5, prob_ref[1:2, :], 0.0)),
                ),
            ),
        ),
    )
    meta = meta.astype(bf16)
    for copy in range(out_ref.shape[0]):
        out_ref[copy, 0:rows, :] = tok_ref[...]
        out_ref[copy, rows : rows + meta_rows, :] = meta


def selection(meta, inner, capacity, weighted):
    tall = group * capacity
    at = [
        (meta[k : k + 1] * tall + inner * capacity + meta[2 + k : 3 + k]).astype(jnp.int32)
        for k in (0, 1)
    ]
    slots = iota((32 * tall, meta.shape[1]), 0)
    if weighted:
        picked = jnp.where(slots == at[0], meta[4:5], jnp.where(slots == at[1], meta[5:6], 0.0))
    else:
        picked = jnp.where((slots == at[0]) | (slots == at[1]), 1.0, 0.0)
    return picked.astype(bf16)


def block_meta(gathered_ref, block, rows):
    return gathered_ref[block, rows : rows + meta_rows, :].astype(f32)


def dispatch(gathered_ref, out_ref):
    blocks, rows = gathered_ref.shape[0], gathered_ref.shape[1] - meta_rows
    capacity = out_ref.shape[2] // blocks
    tall = group * capacity
    for g in range(blocks // group):
        total = 0.0
        for inner in range(group):
            block = g * group + inner
            chosen = selection(block_meta(gathered_ref, block, rows), inner, capacity, False)
            total = total + jnp.dot(
                chosen, gathered_ref[block, 0:rows, :], preferred_element_type=f32
            )
        total = total.astype(bf16)
        for e in range(out_ref.shape[1]):
            for pair in range(out_ref.shape[0]):
                out_ref[pair, e, g * tall : (g + 1) * tall, :] = total[e * tall : (e + 1) * tall]


def dispatch_grad(gathered_ref, grad_ref, out_ref):
    blocks, rows = gathered_ref.shape[0], gathered_ref.shape[1] - meta_rows
    capacity = out_ref.shape[2] // blocks
    tall = group * capacity
    for g in range(blocks // group):
        total = 0.0
        for inner in range(group):
            block = g * group + inner
            chosen = selection(block_meta(gathered_ref, block, rows), inner, capacity, True)
            total = total + contract(chosen, grad_ref[block, 0:rows, :], 1, 1)
        total = total.astype(bf16)
        for e in range(out_ref.shape[1]):
            for pair in range(out_ref.shape[0]):
                out_ref[pair, e, g * tall : (g + 1) * tall, :] = total[e * tall : (e + 1) * tall]


def expert(rows_ref, gain_ref, gate_ref, up_ref, down_ref, out_ref, hidden_ref):
    pairs, parts, half, width = rows_ref.shape
    values = jnp.concatenate(
        [
            jnp.concatenate([rows_ref[h, p] for p in range(parts)], axis=1)
            for h in range(pairs)
        ],
        axis=0,
    ).astype(f32)
    mean_sq = jnp.sum(values * values, axis=1, keepdims=True) / (parts * width)
    normed = (values * lax.rsqrt(mean_sq + eps_norm) * gain_ref[...]).astype(bf16)
    gate_val = jnp.dot(normed, gate_ref[...], preferred_element_type=f32)
    up_val = jnp.dot(normed, up_ref[...], preferred_element_type=f32)
    hidden = (gate_val / (1.0 + jnp.exp(-gate_val)) * up_val).astype(bf16)
    hidden_ref[...] = hidden
    product = jnp.dot(hidden, down_ref[...], preferred_element_type=f32)
    for h in range(pairs):
        for p in range(parts):
            out_ref[h, p] = product[
                h * half : (h + 1) * half, p * width : (p + 1) * width
            ].astype(bf16)


def combine(gathered_ref, back_ref, out_ref):
    blocks, rows = gathered_ref.shape[0], gathered_ref.shape[1] - meta_rows
    capacity = back_ref.shape[2] // blocks
    tall = group * capacity
    for g in range(blocks // group):
        back = jnp.concatenate(
            [
                sum(
                    back_ref[pair, e, g * tall : (g + 1) * tall, :].astype(f32)
                    for pair in range(back_ref.shape[0])
                )
                for e in range(back_ref.shape[1])
            ],
            axis=0,
        )
        back = back.T.astype(bf16)
        for inner in range(group):
            block = g * group + inner
            chosen = selection(block_meta(gathered_ref, block, rows), inner, capacity, True)
            out_ref[block] = jnp.dot(back, chosen, preferred_element_type=f32).astype(bf16)


def project(pieces_ref, tok_ref, weight_ref, state_ref, out_ref):
    total = tok_ref[...].astype(f32).T
    for p in range(pieces_ref.shape[0]):
        total = total + pieces_ref[p].astype(f32)
    state = total.astype(bf16)
    state_ref[...] = state
    out_ref[...] = contract(weight_ref[...], state, 0, 0).astype(bf16)


def form_cotangent(pieces_ref, target_ref, mask_ref, out_ref):
    total = pieces_ref[0].astype(f32)
    for p in range(1, pieces_ref.shape[0]):
        total = total + pieces_ref[p].astype(f32)
    target = target_ref[...].astype(f32)
    scaled = mask_ref[...].astype(f32) * (total - target) * target.shape[1] ** (-0.5)
    scaled = scaled.astype(bf16)
    for p in range(out_ref.shape[0]):
        out_ref[p] = scaled


def gradients(cot_ref, state_ref, partner_ref, weight_ref, out_ref):
    width = weight_ref.shape[0]
    me = lax.axis_index("near")
    state_grad = jnp.dot(
        weight_ref[...], cot_ref[me], preferred_element_type=f32
    ).astype(bf16)
    columns = cot_ref.shape[1] // (2 * out_ref.shape[0])
    for q in range(out_ref.shape[0]):
        out_ref[q, 0:width, :] = state_grad
        at = pl.ds(pl.multiple_of((2 * q + me) * columns, columns), columns)
        part = contract(state_ref[...], cot_ref[me, at, :], 1, 1)
        part = part + contract(partner_ref[...], cot_ref[1 - me, at, :], 1, 1)
        out_ref[q, width:, :] = part.astype(bf16)


def down_gradient(hidden_ref, rows_ref, parts_ref, out_ref, key_value_ref):
    key_value_ref[...] = sum(
        parts_ref[q, key_value_ref.shape[0] :, :].astype(f32) for q in range(parts_ref.shape[0])
    )
    hidden = hidden_ref[...].astype(f32).T.astype(bf16)
    pairs, parts, half, width = rows_ref.shape
    for p in range(parts):
        rows = jnp.concatenate([rows_ref[h, p] for h in range(pairs)], axis=0)
        out_ref[:, p * width : (p + 1) * width] = jnp.dot(
            hidden, rows, preferred_element_type=f32
        ).astype(bf16)


def per_device(
    tokens,
    norm_gain,
    routes,
    route_prob,
    gate_weight,
    up_weight,
    down_weight,
    key_value_weight,
    key_value_target,
    concept_mask,
):
    rows, width = tokens.shape
    experts = lax.axis_size("expert")
    far, near = lax.axis_size("far"), lax.axis_size("near")
    blocks = far * near
    capacity = 5 * rows * routes.shape[1] // (4 * experts)
    keys = key_value_weight.shape[1]

    def shape(*dims, dtype=bf16):
        return jax.ShapeDtypeStruct(dims, dtype)

    def exchange(value, axis):
        return lax.all_to_all(value, axis, split_axis=0, concat_axis=0, tiled=True)

    packed = call(
        prepare, shape(far, rows + meta_rows, width), tokens, routes.T, route_prob.T
    )
    gathered = exchange(packed, "far")
    slots = shape(near, experts, far * capacity, width)
    spots = (near * experts, far * capacity, width)

    def route(value):
        return exchange(value.reshape(spots), ("near", "expert")).reshape(slots.shape)

    arrived = route(call(dispatch, slots, gathered))
    out_rows, hidden = call(
        expert,
        [slots, shape(blocks * capacity, gate_weight.shape[2])],
        arrived,
        norm_gain[None, :],
        gate_weight[0],
        up_weight[0],
        down_weight[0],
        limit=24,
    )
    returned = route(out_rows)
    mixed = exchange(call(combine, shape(far, width, rows), gathered, returned), "far")
    state, proj = call(
        project, [shape(width, rows), shape(keys, rows)], mixed, tokens, key_value_weight
    )
    proj = exchange(proj.reshape(experts, keys // experts, rows), "expert")
    partner = lax.ppermute(state, "near", [(0, 1), (1, 0)])
    spread = call(
        form_cotangent,
        shape(near * experts, *proj.shape[1:]),
        proj,
        key_value_target.T,
        concept_mask[None, :],
    )
    cotangents = exchange(spread, ("near", "expert")).reshape(near, keys, rows)
    sent = call(
        gradients,
        shape(far, 2 * width, rows),
        cotangents,
        state,
        partner,
        key_value_weight,
    )
    all_grads = exchange(sent, "far")
    landed = route(call(dispatch_grad, slots, gathered, all_grads))
    down_grad, key_value_grad = call(
        down_gradient,
        [shape(*down_weight.shape[1:]), shape(width, keys // blocks, dtype=f32)],
        hidden,
        landed,
        all_grads,
    )
    return (down_grad[None], key_value_grad)


def solution(mesh):
    blocks, experts = mesh.devices.shape
    fine = Mesh(mesh.devices.reshape(blocks // 2, 2, experts), ("far", "near", "expert"))
    dp = ("far", "near")
    placed = (
        P(dp, "expert"),
        P(),
        P(dp, None),
        P(dp, None),
        P("expert", None, dp),
        P("expert", None, dp),
        P("expert", dp, None),
        P("expert", None),
        P(dp, "expert"),
        P(dp),
    )
    return jax.shard_map(
        per_device,
        mesh=fine,
        in_specs=placed,
        out_specs=(P("expert", dp, None), P("expert", dp)),
        check_vma=False,
    )
```

```python
import jax
import jax.numpy as jnp
from jax import lax
from jax.experimental import pallas as pl
from jax.experimental.pallas import tpu as pltpu
from jax.sharding import Mesh
from jax.sharding import PartitionSpec as P

f32 = jnp.float32
bf16 = jnp.bfloat16
eps_norm = 1e-06
meta_rows = 8
group = 4


def call(body, outs, *operands, limit=16):
    vmem = pl.BlockSpec(memory_space=pltpu.VMEM)
    single = not isinstance(outs, (list, tuple))
    return pl.pallas_call(
        body,
        out_shape=outs,
        in_specs=[vmem] * len(operands),
        out_specs=vmem if single else [vmem] * len(outs),
        compiler_params=pltpu.CompilerParams(vmem_limit_bytes=limit * 1024 * 1024),
    )(*operands)


def iota(shape, axis):
    return lax.broadcasted_iota(jnp.int32, shape, axis)


def contract(a, b, da, db):
    return lax.dot_general(a, b, (((da,), (db,)), ((), ())), preferred_element_type=f32)


def prepare(tok_ref, choices_ref, out_ref):
    rows, experts = tok_ref.shape[0], 32
    first, second = choices_ref[0:1, :], choices_ref[1:2, :]
    names = iota((experts, rows), 0).astype(f32)
    is_first, is_second = names == first, names == second
    named = jnp.where(is_first | is_second, 1.0, 0.0).astype(bf16)
    earlier = jnp.where(iota((rows, rows), 0) < iota((rows, rows), 1), 1.0, 0.0).astype(bf16)
    before = jnp.dot(named, earlier, preferred_element_type=f32)
    slot_first = jnp.sum(jnp.where(is_first, before, 0.0), axis=0, keepdims=True)
    slot_second = jnp.sum(jnp.where(is_second, before, 0.0), axis=0, keepdims=True)
    row = iota((meta_rows, rows), 0)
    meta = jnp.where(
        row == 0,
        first,
        jnp.where(
            row == 1,
            second,
            jnp.where(
                row == 2,
                slot_first,
                jnp.where(
                    row == 3,
                    slot_second,
                    jnp.where(row == 4, choices_ref[2:3, :], jnp.where(row == 5, choices_ref[3:4, :], 0.0)),
                ),
            ),
        ),
    )
    meta = meta.astype(bf16)
    for copy in range(out_ref.shape[0]):
        out_ref[copy, 0:rows, :] = tok_ref[...]
        out_ref[copy, rows : rows + meta_rows, :] = meta


def selection(meta, inner, capacity, weighted):
    tall = group * capacity
    at = [
        (meta[k : k + 1] * tall + inner * capacity + meta[2 + k : 3 + k]).astype(jnp.int32)
        for k in (0, 1)
    ]
    slots = iota((32 * tall, meta.shape[1]), 0)
    if weighted:
        picked = jnp.where(slots == at[0], meta[4:5], jnp.where(slots == at[1], meta[5:6], 0.0))
    else:
        picked = jnp.where((slots == at[0]) | (slots == at[1]), 1.0, 0.0)
    return picked.astype(bf16)


def block_meta(gathered_ref, block, rows):
    return gathered_ref[block, rows : rows + meta_rows, :].astype(f32)


def dispatch(gathered_ref, out_ref):
    blocks, rows = gathered_ref.shape[0], gathered_ref.shape[1] - meta_rows
    capacity = out_ref.shape[2] // blocks
    tall = group * capacity
    for g in range(blocks // group):
        total = 0.0
        for inner in range(group):
            block = g * group + inner
            chosen = selection(block_meta(gathered_ref, block, rows), inner, capacity, False)
            total = total + jnp.dot(
                chosen, gathered_ref[block, 0:rows, :], preferred_element_type=f32
            )
        total = total.astype(bf16)
        for e in range(out_ref.shape[1]):
            for pair in range(out_ref.shape[0]):
                out_ref[pair, e, g * tall : (g + 1) * tall, :] = total[e * tall : (e + 1) * tall]


def dispatch_grad(gathered_ref, grad_ref, out_ref):
    blocks, rows = gathered_ref.shape[0], gathered_ref.shape[1] - meta_rows
    capacity = out_ref.shape[2] // blocks
    tall = group * capacity
    for g in range(blocks // group):
        total = 0.0
        for inner in range(group):
            block = g * group + inner
            chosen = selection(block_meta(gathered_ref, block, rows), inner, capacity, True)
            total = total + contract(chosen, grad_ref[block, 0:rows, :], 1, 1)
        total = total.astype(bf16)
        for e in range(out_ref.shape[1]):
            for pair in range(out_ref.shape[0]):
                out_ref[pair, e, g * tall : (g + 1) * tall, :] = total[e * tall : (e + 1) * tall]


def expert(rows_ref, gain_ref, gate_ref, up_ref, down_ref, out_ref, hidden_ref):
    pairs, parts, half, width = rows_ref.shape
    values = jnp.concatenate(
        [
            jnp.concatenate([rows_ref[h, p] for p in range(parts)], axis=1)
            for h in range(pairs)
        ],
        axis=0,
    ).astype(f32)
    mean_sq = jnp.sum(values * values, axis=1, keepdims=True) / (parts * width)
    normed = (values * lax.rsqrt(mean_sq + eps_norm) * gain_ref[...]).astype(bf16)
    gate_val = jnp.dot(normed, gate_ref[...], preferred_element_type=f32)
    up_val = jnp.dot(normed, up_ref[...], preferred_element_type=f32)
    hidden = (gate_val / (1.0 + jnp.exp(-gate_val)) * up_val).astype(bf16)
    hidden_ref[...] = hidden
    product = jnp.dot(hidden, down_ref[...], preferred_element_type=f32)
    for h in range(pairs):
        for p in range(parts):
            out_ref[h, p] = product[
                h * half : (h + 1) * half, p * width : (p + 1) * width
            ].astype(bf16)


def combine(gathered_ref, back_ref, out_ref):
    blocks, rows = gathered_ref.shape[0], gathered_ref.shape[1] - meta_rows
    capacity = back_ref.shape[2] // blocks
    tall = group * capacity
    for g in range(blocks // group):
        back = jnp.concatenate(
            [
                sum(
                    back_ref[pair, e, g * tall : (g + 1) * tall, :].astype(f32)
                    for pair in range(back_ref.shape[0])
                )
                for e in range(back_ref.shape[1])
            ],
            axis=0,
        )
        back = back.T.astype(bf16)
        for inner in range(group):
            block = g * group + inner
            chosen = selection(block_meta(gathered_ref, block, rows), inner, capacity, True)
            out_ref[block] = jnp.dot(back, chosen, preferred_element_type=f32).astype(bf16)


def project(pieces_ref, tok_ref, weight_ref, state_ref, out_ref):
    total = tok_ref[...].astype(f32).T
    for p in range(pieces_ref.shape[0]):
        total = total + pieces_ref[p].astype(f32)
    state = total.astype(bf16)
    state_ref[...] = state
    out_ref[...] = contract(weight_ref[...], state, 0, 0).astype(bf16)


def form_cotangent(pieces_ref, target_ref, mask_ref, out_ref):
    total = pieces_ref[0].astype(f32)
    for p in range(1, pieces_ref.shape[0]):
        total = total + pieces_ref[p].astype(f32)
    target = target_ref[...].astype(f32)
    scaled = mask_ref[...].astype(f32) * (total - target) * target.shape[1] ** (-0.5)
    scaled = scaled.astype(bf16)
    for p in range(out_ref.shape[0]):
        out_ref[p] = scaled


def gradients(cot_ref, state_ref, partner_ref, weight_ref, out_ref):
    width = weight_ref.shape[0]
    me = lax.axis_index("near")
    state_grad = jnp.dot(
        weight_ref[...], cot_ref[me], preferred_element_type=f32
    ).astype(bf16)
    columns = cot_ref.shape[1] // (2 * out_ref.shape[0])
    for q in range(out_ref.shape[0]):
        out_ref[q, 0:width, :] = state_grad
        at = pl.ds(pl.multiple_of((2 * q + me) * columns, columns), columns)
        part = contract(state_ref[...], cot_ref[me, at, :], 1, 1)
        part = part + contract(partner_ref[...], cot_ref[1 - me, at, :], 1, 1)
        out_ref[q, width:, :] = part.astype(bf16)


def down_gradient(hidden_ref, rows_ref, parts_ref, out_ref, key_value_ref):
    key_value_ref[...] = sum(
        parts_ref[q, key_value_ref.shape[0] :, :].astype(f32) for q in range(parts_ref.shape[0])
    )
    hidden = hidden_ref[...].astype(f32).T.astype(bf16)
    pairs, parts, half, width = rows_ref.shape
    for p in range(parts):
        rows = jnp.concatenate([rows_ref[h, p] for h in range(pairs)], axis=0)
        out_ref[:, p * width : (p + 1) * width] = jnp.dot(
            hidden, rows, preferred_element_type=f32
        ).astype(bf16)


def per_device(
    tokens,
    norm_gain,
    routes,
    route_prob,
    gate_weight,
    up_weight,
    down_weight,
    key_value_weight,
    key_value_target,
    concept_mask,
):
    rows, width = tokens.shape
    experts = lax.axis_size("expert")
    far, near = lax.axis_size("far"), lax.axis_size("near")
    blocks = far * near
    capacity = 5 * rows * routes.shape[1] // (4 * experts)
    keys = key_value_weight.shape[1]

    def shape(*dims, dtype=bf16):
        return jax.ShapeDtypeStruct(dims, dtype)

    def exchange(value, axis):
        return lax.all_to_all(value, axis, split_axis=0, concat_axis=0, tiled=True)

    choices = jnp.concatenate([routes.T.astype(f32), route_prob.T], axis=0)
    packed = call(prepare, shape(far, rows + meta_rows, width), tokens, choices)
    gathered = exchange(packed, "far")
    slots = shape(near, experts, far * capacity, width)
    spots = (near * experts, far * capacity, width)

    def route(value):
        return exchange(value.reshape(spots), ("near", "expert")).reshape(slots.shape)

    arrived = route(call(dispatch, slots, gathered))
    out_rows, hidden = call(
        expert,
        [slots, shape(blocks * capacity, gate_weight.shape[2])],
        arrived,
        norm_gain[None, :],
        gate_weight[0],
        up_weight[0],
        down_weight[0],
        limit=24,
    )
    returned = route(out_rows)
    mixed = exchange(call(combine, shape(far, width, rows), gathered, returned), "far")
    state, proj = call(
        project, [shape(width, rows), shape(keys, rows)], mixed, tokens, key_value_weight
    )
    proj = exchange(proj.reshape(experts, keys // experts, rows), "expert")
    partner = lax.ppermute(state, "near", [(0, 1), (1, 0)])
    proj, partner = lax.optimization_barrier((proj, partner))
    spread = call(
        form_cotangent,
        shape(near * experts, *proj.shape[1:]),
        proj,
        key_value_target.T,
        concept_mask[None, :],
    )
    cotangents = exchange(spread, ("near", "expert")).reshape(near, keys, rows)
    sent = call(
        gradients,
        shape(far, 2 * width, rows),
        cotangents,
        state,
        partner,
        key_value_weight,
    )
    all_grads = exchange(sent, "far")
    landed = route(call(dispatch_grad, slots, gathered, all_grads))
    down_grad, key_value_grad = call(
        down_gradient,
        [shape(*down_weight.shape[1:]), shape(width, keys // blocks, dtype=f32)],
        hidden,
        landed,
        all_grads,
    )
    return (down_grad[None], key_value_grad)


def solution(mesh):
    blocks, experts = mesh.devices.shape
    fine = Mesh(mesh.devices.reshape(blocks // 2, 2, experts), ("far", "near", "expert"))
    dp = ("far", "near")
    placed = (
        P(dp, "expert"),
        P(),
        P(dp, None),
        P(dp, None),
        P("expert", None, dp),
        P("expert", None, dp),
        P("expert", dp, None),
        P("expert", None),
        P(dp, "expert"),
        P(dp),
    )
    return jax.shard_map(
        per_device,
        mesh=fine,
        in_specs=placed,
        out_specs=(P("expert", dp, None), P("expert", dp)),
        check_vma=False,
    )
```

```python
import jax
import jax.numpy as jnp
from jax import lax
from jax.experimental import pallas as pl
from jax.experimental.pallas import tpu as pltpu
from jax.sharding import Mesh
from jax.sharding import PartitionSpec as P

f32 = jnp.float32
bf16 = jnp.bfloat16
eps_norm = 1e-06
meta_rows = 8
group = 4


def call(body, outs, *operands, limit=16):
    vmem = pl.BlockSpec(memory_space=pltpu.VMEM)
    single = not isinstance(outs, (list, tuple))
    return pl.pallas_call(
        body,
        out_shape=outs,
        in_specs=[vmem] * len(operands),
        out_specs=vmem if single else [vmem] * len(outs),
        compiler_params=pltpu.CompilerParams(vmem_limit_bytes=limit * 1024 * 1024),
    )(*operands)


def iota(shape, axis):
    return lax.broadcasted_iota(jnp.int32, shape, axis)


def contract(a, b, da, db):
    return lax.dot_general(a, b, (((da,), (db,)), ((), ())), preferred_element_type=f32)


def prepare(tok_ref, choices_ref, out_ref):
    rows, experts = tok_ref.shape[0], 32
    first, second = choices_ref[0:1, :], choices_ref[1:2, :]
    names = iota((experts, rows), 0).astype(f32)
    is_first, is_second = names == first, names == second
    named = jnp.where(is_first | is_second, 1.0, 0.0).astype(bf16)
    earlier = jnp.where(iota((rows, rows), 0) < iota((rows, rows), 1), 1.0, 0.0).astype(bf16)
    before = jnp.dot(named, earlier, preferred_element_type=f32)
    slot_first = jnp.sum(jnp.where(is_first, before, 0.0), axis=0, keepdims=True)
    slot_second = jnp.sum(jnp.where(is_second, before, 0.0), axis=0, keepdims=True)
    row = iota((meta_rows, rows), 0)
    meta = jnp.where(
        row == 0,
        first,
        jnp.where(
            row == 1,
            second,
            jnp.where(
                row == 2,
                slot_first,
                jnp.where(
                    row == 3,
                    slot_second,
                    jnp.where(row == 4, choices_ref[2:3, :], jnp.where(row == 5, choices_ref[3:4, :], 0.0)),
                ),
            ),
        ),
    )
    meta = meta.astype(bf16)
    for copy in range(out_ref.shape[0]):
        out_ref[copy, 0:rows, :] = tok_ref[...]
        out_ref[copy, rows : rows + meta_rows, :] = meta


def selection(meta, inner, capacity, weighted):
    tall = group * capacity
    at = [
        (meta[k : k + 1] * tall + inner * capacity + meta[2 + k : 3 + k]).astype(jnp.int32)
        for k in (0, 1)
    ]
    slots = iota((32 * tall, meta.shape[1]), 0)
    if weighted:
        picked = jnp.where(slots == at[0], meta[4:5], jnp.where(slots == at[1], meta[5:6], 0.0))
    else:
        picked = jnp.where((slots == at[0]) | (slots == at[1]), 1.0, 0.0)
    return picked.astype(bf16)


def block_meta(gathered_ref, block, rows):
    return gathered_ref[block, rows : rows + meta_rows, :].astype(f32)


def dispatch(gathered_ref, out_ref):
    blocks, rows = gathered_ref.shape[0], gathered_ref.shape[1] - meta_rows
    capacity = out_ref.shape[2] // blocks
    tall = group * capacity
    for g in range(blocks // group):
        total = 0.0
        for inner in range(group):
            block = g * group + inner
            chosen = selection(block_meta(gathered_ref, block, rows), inner, capacity, False)
            total = total + jnp.dot(
                chosen, gathered_ref[block, 0:rows, :], preferred_element_type=f32
            )
        total = total.astype(bf16)
        for e in range(out_ref.shape[1]):
            for pair in range(out_ref.shape[0]):
                out_ref[pair, e, g * tall : (g + 1) * tall, :] = total[e * tall : (e + 1) * tall]


def dispatch_grad(gathered_ref, grad_ref, out_ref):
    blocks, rows = gathered_ref.shape[0], gathered_ref.shape[1] - meta_rows
    capacity = out_ref.shape[2] // blocks
    tall = group * capacity
    for g in range(blocks // group):
        total = 0.0
        for inner in range(group):
            block = g * group + inner
            chosen = selection(block_meta(gathered_ref, block, rows), inner, capacity, True)
            total = total + contract(chosen, grad_ref[block, 0:rows, :], 1, 1)
        total = total.astype(bf16)
        for e in range(out_ref.shape[1]):
            for pair in range(out_ref.shape[0]):
                out_ref[pair, e, g * tall : (g + 1) * tall, :] = total[e * tall : (e + 1) * tall]


def expert(rows_ref, gain_ref, gate_ref, up_ref, down_ref, out_ref, hidden_ref):
    pairs, parts, half, width = rows_ref.shape
    values = jnp.concatenate(
        [
            jnp.concatenate([rows_ref[h, p] for p in range(parts)], axis=1)
            for h in range(pairs)
        ],
        axis=0,
    ).astype(f32)
    mean_sq = jnp.sum(values * values, axis=1, keepdims=True) / (parts * width)
    normed = (values * lax.rsqrt(mean_sq + eps_norm) * gain_ref[...]).astype(bf16)
    gate_val = jnp.dot(normed, gate_ref[...], preferred_element_type=f32)
    up_val = jnp.dot(normed, up_ref[...], preferred_element_type=f32)
    hidden = (gate_val / (1.0 + jnp.exp(-gate_val)) * up_val).astype(bf16)
    hidden_ref[...] = hidden
    product = jnp.dot(hidden, down_ref[...], preferred_element_type=f32)
    for h in range(pairs):
        for p in range(parts):
            out_ref[h, p] = product[
                h * half : (h + 1) * half, p * width : (p + 1) * width
            ].astype(bf16)


def combine(gathered_ref, back_ref, out_ref):
    blocks, rows = gathered_ref.shape[0], gathered_ref.shape[1] - meta_rows
    capacity = back_ref.shape[2] // blocks
    tall = group * capacity
    for g in range(blocks // group):
        back = jnp.concatenate(
            [
                sum(
                    back_ref[pair, e, g * tall : (g + 1) * tall, :].astype(f32)
                    for pair in range(back_ref.shape[0])
                )
                for e in range(back_ref.shape[1])
            ],
            axis=0,
        )
        back = back.T.astype(bf16)
        for inner in range(group):
            block = g * group + inner
            chosen = selection(block_meta(gathered_ref, block, rows), inner, capacity, True)
            out_ref[block] = jnp.dot(back, chosen, preferred_element_type=f32).astype(bf16)


def project(pieces_ref, tok_ref, weight_ref, state_ref, out_ref):
    total = tok_ref[...].astype(f32).T
    for p in range(pieces_ref.shape[0]):
        total = total + pieces_ref[p].astype(f32)
    state = total.astype(bf16)
    state_ref[...] = state
    out_ref[...] = contract(weight_ref[...], state, 0, 0).astype(bf16)


def form_cotangent(pieces_ref, target_ref, mask_ref, out_ref):
    total = pieces_ref[0].astype(f32)
    for p in range(1, pieces_ref.shape[0]):
        total = total + pieces_ref[p].astype(f32)
    target = target_ref[...].astype(f32)
    scaled = mask_ref[...].astype(f32) * (total - target) * target.shape[1] ** (-0.5)
    scaled = scaled.astype(bf16)
    for p in range(out_ref.shape[0]):
        out_ref[p] = scaled


def gradients(cot_ref, state_ref, partner_ref, weight_ref, out_ref, *part_refs):
    me, place = lax.axis_index("near"), lax.axis_index("far")
    state_grad = jnp.dot(
        weight_ref[...], cot_ref[me], preferred_element_type=f32
    ).astype(bf16)
    peers = out_ref.shape[0]
    columns = cot_ref.shape[1] // (2 * peers)
    for d in range(peers):
        out_ref[d] = state_grad
        plane = 2 * ((place + d) % peers) + me
        at = pl.ds(pl.multiple_of(plane * columns, columns), columns)
        part = contract(state_ref[...], cot_ref[me, at, :], 1, 1)
        part = part + contract(partner_ref[...], cot_ref[1 - me, at, :], 1, 1)
        part_refs[d][...] = part.astype(bf16)


def down_gradient(hidden_ref, rows_ref, *refs):
    part_refs, (out_ref, key_value_ref) = refs[:-2], refs[-2:]
    key_value_ref[...] = sum(part[...].astype(f32) for part in part_refs)
    hidden = hidden_ref[...].astype(f32).T.astype(bf16)
    pairs, parts, half, width = rows_ref.shape
    for p in range(parts):
        rows = jnp.concatenate([rows_ref[h, p] for h in range(pairs)], axis=0)
        out_ref[:, p * width : (p + 1) * width] = jnp.dot(
            hidden, rows, preferred_element_type=f32
        ).astype(bf16)


def per_device(
    tokens,
    norm_gain,
    routes,
    route_prob,
    gate_weight,
    up_weight,
    down_weight,
    key_value_weight,
    key_value_target,
    concept_mask,
):
    rows, width = tokens.shape
    experts = lax.axis_size("expert")
    far, near = lax.axis_size("far"), lax.axis_size("near")
    blocks = far * near
    capacity = 5 * rows * routes.shape[1] // (4 * experts)
    keys = key_value_weight.shape[1]

    def shape(*dims, dtype=bf16):
        return jax.ShapeDtypeStruct(dims, dtype)

    def exchange(value, axis):
        return lax.all_to_all(value, axis, split_axis=0, concat_axis=0, tiled=True)

    choices = jnp.concatenate([routes.T.astype(f32), route_prob.T], axis=0)
    packed = call(prepare, shape(far, rows + meta_rows, width), tokens, choices)
    gathered = exchange(packed, "far")
    slots = shape(near, experts, far * capacity, width)
    spots = (near * experts, far * capacity, width)

    def route(value):
        return exchange(value.reshape(spots), ("near", "expert")).reshape(slots.shape)

    arrived = route(call(dispatch, slots, gathered))
    out_rows, hidden = call(
        expert,
        [slots, shape(blocks * capacity, gate_weight.shape[2])],
        arrived,
        norm_gain[None, :],
        gate_weight[0],
        up_weight[0],
        down_weight[0],
        limit=24,
    )
    returned = route(out_rows)
    mixed = exchange(call(combine, shape(far, width, rows), gathered, returned), "far")
    state, proj = call(
        project, [shape(width, rows), shape(keys, rows)], mixed, tokens, key_value_weight
    )
    proj = exchange(proj.reshape(experts, keys // experts, rows), "expert")
    partner = lax.ppermute(state, "near", [(0, 1), (1, 0)])
    proj, partner = lax.optimization_barrier((proj, partner))
    spread = call(
        form_cotangent,
        shape(near * experts, *proj.shape[1:]),
        proj,
        key_value_target.T,
        concept_mask[None, :],
    )
    cotangents = exchange(spread, ("near", "expert")).reshape(near, keys, rows)
    sent, *parts = call(
        gradients,
        [shape(far, width, rows)] + [shape(width, keys // blocks)] * far,
        cotangents,
        state,
        partner,
        key_value_weight,
    )
    all_grads = exchange(sent, "far")
    for d in range(1, far):
        parts[d] = lax.ppermute(parts[d], "far", [(i, (i + d) % far) for i in range(far)])
    landed = route(call(dispatch_grad, slots, gathered, all_grads))
    down_grad, key_value_grad = call(
        down_gradient,
        [shape(*down_weight.shape[1:]), shape(width, keys // blocks, dtype=f32)],
        hidden,
        landed,
        *parts,
    )
    return (down_grad[None], key_value_grad)


def solution(mesh):
    blocks, experts = mesh.devices.shape
    fine = Mesh(mesh.devices.reshape(blocks // 2, 2, experts), ("far", "near", "expert"))
    dp = ("far", "near")
    placed = (
        P(dp, "expert"),
        P(),
        P(dp, None),
        P(dp, None),
        P("expert", None, dp),
        P("expert", None, dp),
        P("expert", dp, None),
        P("expert", None),
        P(dp, "expert"),
        P(dp),
    )
    return jax.shard_map(
        per_device,
        mesh=fine,
        in_specs=placed,
        out_specs=(P("expert", dp, None), P("expert", dp)),
        check_vma=False,
    )
```

```python
import jax
import jax.numpy as jnp
from jax import lax
from jax.experimental import pallas as pl
from jax.experimental.pallas import tpu as pltpu
from jax.sharding import Mesh
from jax.sharding import PartitionSpec as P

f32 = jnp.float32
bf16 = jnp.bfloat16
eps_norm = 1e-06
meta_rows = 8
group = 4


def call(body, outs, *operands, limit=16):
    vmem = pl.BlockSpec(memory_space=pltpu.VMEM)
    single = not isinstance(outs, (list, tuple))
    return pl.pallas_call(
        body,
        out_shape=outs,
        in_specs=[vmem] * len(operands),
        out_specs=vmem if single else [vmem] * len(outs),
        compiler_params=pltpu.CompilerParams(vmem_limit_bytes=limit * 1024 * 1024),
    )(*operands)


def iota(shape, axis):
    return lax.broadcasted_iota(jnp.int32, shape, axis)


def contract(a, b, da, db):
    return lax.dot_general(a, b, (((da,), (db,)), ((), ())), preferred_element_type=f32)


def prepare(tok_ref, routes_ref, prob_ref, out_ref):
    rows, experts = tok_ref.shape[0], 32
    routes = routes_ref[...].astype(f32)
    first, second = routes[0:1, :], routes[1:2, :]
    names = iota((experts, rows), 0).astype(f32)
    is_first, is_second = names == first, names == second
    named = jnp.where(is_first | is_second, 1.0, 0.0).astype(bf16)
    earlier = jnp.where(iota((rows, rows), 0) < iota((rows, rows), 1), 1.0, 0.0).astype(bf16)
    before = jnp.dot(named, earlier, preferred_element_type=f32)
    slot_first = jnp.sum(jnp.where(is_first, before, 0.0), axis=0, keepdims=True)
    slot_second = jnp.sum(jnp.where(is_second, before, 0.0), axis=0, keepdims=True)
    row = iota((meta_rows, rows), 0)
    meta = jnp.where(
        row == 0,
        first,
        jnp.where(
            row == 1,
            second,
            jnp.where(
                row == 2,
                slot_first,
                jnp.where(
                    row == 3,
                    slot_second,
                    jnp.where(row == 4, prob_ref[0:1, :], jnp.where(row == 5, prob_ref[1:2, :], 0.0)),
                ),
            ),
        ),
    )
    meta = meta.astype(bf16)
    for copy in range(out_ref.shape[0]):
        out_ref[copy, 0:rows, :] = tok_ref[...]
        out_ref[copy, rows : rows + meta_rows, :] = meta


def selection(meta, inner, capacity, weighted):
    tall = group * capacity
    at = [
        (meta[k : k + 1] * tall + inner * capacity + meta[2 + k : 3 + k]).astype(jnp.int32)
        for k in (0, 1)
    ]
    slots = iota((32 * tall, meta.shape[1]), 0)
    if weighted:
        picked = jnp.where(slots == at[0], meta[4:5], jnp.where(slots == at[1], meta[5:6], 0.0))
    else:
        picked = jnp.where((slots == at[0]) | (slots == at[1]), 1.0, 0.0)
    return picked.astype(bf16)


def block_meta(gathered_ref, block, rows):
    return gathered_ref[block, rows : rows + meta_rows, :].astype(f32)


def dispatch(gathered_ref, out_ref):
    blocks, rows = gathered_ref.shape[0], gathered_ref.shape[1] - meta_rows
    capacity = out_ref.shape[2] // blocks
    tall = group * capacity
    for g in range(blocks // group):
        total = 0.0
        for inner in range(group):
            block = g * group + inner
            chosen = selection(block_meta(gathered_ref, block, rows), inner, capacity, False)
            total = total + jnp.dot(
                chosen, gathered_ref[block, 0:rows, :], preferred_element_type=f32
            )
        total = total.astype(bf16)
        for e in range(out_ref.shape[1]):
            for pair in range(out_ref.shape[0]):
                out_ref[pair, e, g * tall : (g + 1) * tall, :] = total[e * tall : (e + 1) * tall]


def dispatch_grad(gathered_ref, grad_ref, out_ref):
    blocks, rows = gathered_ref.shape[0], gathered_ref.shape[1] - meta_rows
    capacity = out_ref.shape[2] // blocks
    tall = group * capacity
    for g in range(blocks // group):
        total = 0.0
        for inner in range(group):
            block = g * group + inner
            chosen = selection(block_meta(gathered_ref, block, rows), inner, capacity, True)
            total = total + contract(chosen, grad_ref[block, 0:rows, :], 1, 1)
        total = total.astype(bf16)
        for e in range(out_ref.shape[1]):
            for pair in range(out_ref.shape[0]):
                out_ref[pair, e, g * tall : (g + 1) * tall, :] = total[e * tall : (e + 1) * tall]


def expert(rows_ref, gain_ref, gate_ref, up_ref, down_ref, out_ref, hidden_ref):
    pairs, parts, half, width = rows_ref.shape
    values = jnp.concatenate(
        [
            jnp.concatenate([rows_ref[h, p] for p in range(parts)], axis=1)
            for h in range(pairs)
        ],
        axis=0,
    ).astype(f32)
    mean_sq = jnp.sum(values * values, axis=1, keepdims=True) / (parts * width)
    normed = (values * lax.rsqrt(mean_sq + eps_norm) * gain_ref[...]).astype(bf16)
    gate_val = jnp.dot(normed, gate_ref[...], preferred_element_type=f32)
    up_val = jnp.dot(normed, up_ref[...], preferred_element_type=f32)
    hidden = (gate_val / (1.0 + jnp.exp(-gate_val)) * up_val).astype(bf16)
    hidden_ref[...] = hidden
    product = jnp.dot(hidden, down_ref[...], preferred_element_type=f32)
    for h in range(pairs):
        for p in range(parts):
            out_ref[h, p] = product[
                h * half : (h + 1) * half, p * width : (p + 1) * width
            ].astype(bf16)


def combine(gathered_ref, back_ref, out_ref):
    blocks, rows = gathered_ref.shape[0], gathered_ref.shape[1] - meta_rows
    capacity = back_ref.shape[2] // blocks
    tall = group * capacity
    for g in range(blocks // group):
        back = jnp.concatenate(
            [
                sum(
                    back_ref[pair, e, g * tall : (g + 1) * tall, :].astype(f32)
                    for pair in range(back_ref.shape[0])
                )
                for e in range(back_ref.shape[1])
            ],
            axis=0,
        )
        back = back.T.astype(bf16)
        for inner in range(group):
            block = g * group + inner
            chosen = selection(block_meta(gathered_ref, block, rows), inner, capacity, True)
            out_ref[block] = jnp.dot(back, chosen, preferred_element_type=f32).astype(bf16)


def project(pieces_ref, tok_ref, weight_ref, state_ref, out_ref):
    total = tok_ref[...].astype(f32).T
    for p in range(pieces_ref.shape[0]):
        total = total + pieces_ref[p].astype(f32)
    state = total.astype(bf16)
    state_ref[...] = state
    out_ref[...] = contract(weight_ref[...], state, 0, 0).astype(bf16)


def form_cotangent(pieces_ref, target_ref, mask_ref, out_ref):
    total = pieces_ref[0].astype(f32)
    for p in range(1, pieces_ref.shape[0]):
        total = total + pieces_ref[p].astype(f32)
    target = target_ref[...].astype(f32)
    scaled = mask_ref[...].astype(f32) * (total - target) * target.shape[1] ** (-0.5)
    scaled = scaled.astype(bf16)
    for p in range(out_ref.shape[0]):
        out_ref[p] = scaled


def gradients(cot_ref, state_ref, partner_ref, weight_ref, out_ref):
    width = weight_ref.shape[0]
    me = lax.axis_index("near")
    state_grad = jnp.dot(
        weight_ref[...], cot_ref[me], preferred_element_type=f32
    ).astype(bf16)
    columns = cot_ref.shape[1] // (2 * out_ref.shape[0])
    for q in range(out_ref.shape[0]):
        out_ref[q, 0:width, :] = state_grad
        at = pl.ds(pl.multiple_of((2 * q + me) * columns, columns), columns)
        part = contract(state_ref[...], cot_ref[me, at, :], 1, 1)
        part = part + contract(partner_ref[...], cot_ref[1 - me, at, :], 1, 1)
        out_ref[q, width:, :] = part.astype(bf16)


def down_gradient(hidden_ref, rows_ref, parts_ref, out_ref, key_value_ref):
    key_value_ref[...] = sum(
        parts_ref[q, key_value_ref.shape[0] :, :].astype(f32) for q in range(parts_ref.shape[0])
    )
    hidden = hidden_ref[...].astype(f32).T.astype(bf16)
    pairs, parts, half, width = rows_ref.shape
    for p in range(parts):
        rows = jnp.concatenate([rows_ref[h, p] for h in range(pairs)], axis=0)
        out_ref[:, p * width : (p + 1) * width] = jnp.dot(
            hidden, rows, preferred_element_type=f32
        ).astype(bf16)


def per_device(
    tokens,
    norm_gain,
    routes,
    route_prob,
    gate_weight,
    up_weight,
    down_weight,
    key_value_weight,
    key_value_target,
    concept_mask,
):
    rows, width = tokens.shape
    experts = lax.axis_size("expert")
    far, near = lax.axis_size("far"), lax.axis_size("near")
    blocks = far * near
    capacity = 5 * rows * routes.shape[1] // (4 * experts)
    keys = key_value_weight.shape[1]

    def shape(*dims, dtype=bf16):
        return jax.ShapeDtypeStruct(dims, dtype)

    def exchange(value, axis):
        return lax.all_to_all(value, axis, split_axis=0, concat_axis=0, tiled=True)

    packed = call(prepare, shape(far, rows + meta_rows, width), tokens, routes.T, route_prob.T)
    gathered = exchange(packed, "far")
    slots = shape(near, experts, far * capacity, width)
    spots = (near * experts, far * capacity, width)

    def route(value):
        return exchange(value.reshape(spots), ("near", "expert")).reshape(slots.shape)

    arrived = route(call(dispatch, slots, gathered))
    out_rows, hidden = call(
        expert,
        [slots, shape(blocks * capacity, gate_weight.shape[2])],
        arrived,
        norm_gain[None, :],
        gate_weight[0],
        up_weight[0],
        down_weight[0],
        limit=24,
    )
    returned = route(out_rows)
    mixed = exchange(call(combine, shape(far, width, rows), gathered, returned), "far")
    state, proj = call(
        project, [shape(width, rows), shape(keys, rows)], mixed, tokens, key_value_weight
    )
    proj = exchange(proj.reshape(experts, keys // experts, rows), "expert")
    partner = lax.ppermute(state, "near", [(0, 1), (1, 0)])
    spread = call(
        form_cotangent,
        shape(near * experts, *proj.shape[1:]),
        proj,
        key_value_target.T,
        concept_mask[None, :],
    )
    cotangents = exchange(spread, ("near", "expert")).reshape(near, keys, rows)
    sent = call(
        gradients,
        shape(far, 2 * width, rows),
        cotangents,
        state,
        partner,
        key_value_weight,
    )
    all_grads = exchange(sent, "far")
    landed = route(call(dispatch_grad, slots, gathered, all_grads))
    down_grad, key_value_grad = call(
        down_gradient,
        [shape(*down_weight.shape[1:]), shape(width, keys // blocks, dtype=f32)],
        hidden,
        landed,
        all_grads,
    )
    return (down_grad[None], key_value_grad)


def solution(mesh):
    blocks, experts = mesh.devices.shape
    fine = Mesh(mesh.devices.reshape(blocks // 2, 2, experts), ("far", "near", "expert"))
    dp = ("far", "near")
    placed = (
        P(dp, "expert"),
        P(),
        P(dp, None),
        P(dp, None),
        P("expert", None, dp),
        P("expert", None, dp),
        P("expert", dp, None),
        P("expert", None),
        P(dp, "expert"),
        P(dp),
    )
    return jax.shard_map(
        per_device,
        mesh=fine,
        in_specs=placed,
        out_specs=(P("expert", dp, None), P("expert", dp)),
        check_vma=False,
    )
```
